256 devices in a mesh: dp: 16 (over y_lo, x, core), supp: 16 (over y_hi, z).
Axes of the slice: x: 4, y: 4 (y_hi: 2, y_lo: 2; y = y_hi * 2 + y_lo), z: 8, core: 2. Of those that a mesh axis runs over, the one named last changes fastest.
Arguments:
- support_points: float32 [16384, 256], P('supp'), may hold values from -9 to 9, as said below
- data_points: float32 [32768, 256], P('dp'), may hold values from -9 to 9, as said below
- data_weight: float32 [32768], P('dp'), may hold values from 0.5 to 5
Outputs:
- support_out: float32 [16384, 256], P('supp')
The draws below stay inside these ranges and needn't reach their ends.
Inputs may be any that keep to these rules, and one draw needn't show every extreme that they name: `support_points`: finite points; coordinates within the stated range. `data_points`: finite points; coordinates within the stated range.
All inputs are finite; a program needn't handle non-finite values.
Results may differ from the reference program's by a relative error of at most 0.0003.
Values sent between devices are 32-bit elements; how exact they have to be, the bound alone decides.
No kernel may reach another device: no remote copies, remote signals or barrier semaphores. Data moves between devices by JAX's collectives and lax.ppermute only.
A program may use at most 64 MiB of HBM per device.

```python
import math
import jax
import jax.numpy as jnp
from jax import lax

D = 256
M_DEV = 1024
ITERS = 2
OUTER = 2
M = 16384
N = 32768
N_SUPP = 16


def drawn_cloud(key, count, width):
    return jnp.clip(jax.random.normal(jax.random.fold_in(key, 5), (count, width), jnp.float32), -6.0, 6.0)


def draw_support_points(key, part):
    return drawn_cloud(jax.random.fold_in(key, 101), M, D)


def draw_data_points(key, part):
    return drawn_cloud(jax.random.fold_in(key, 202), N, D)


def shard_levels(key, dims, cuts, least, largest):
    def one(position, shards_of):
        steps = jax.random.uniform(jax.random.fold_in(jax.random.fold_in(key, 6), position), (shards_of,), jnp.float32, least / len(cuts), largest / len(cuts))
        return jnp.repeat(jnp.exp(steps), dims[position] // shards_of).reshape((-1,) + (1,) * (len(dims) - position - 1))

    gain = one(*cuts[0])
    for cut in cuts[1:]:
        gain = gain * one(*cut)
    return gain


def setup_inputs(seed: int = 0) -> dict:
    keys = jax.random.split(jax.random.key(seed), 4)
    support_points = draw_support_points(jax.random.fold_in(keys[3], 71), 0)
    data_points = draw_data_points(jax.random.fold_in(keys[3], 71), 0)
    data_weight = jnp.clip(jnp.exp(math.log(5.0) - 2.3025851 * jax.random.uniform(keys[2], (N,), jnp.float32) ** shard_levels(keys[2], (N,), ((0, 16),), -0.2, 0.2)), 0.5, 5.0)
    return {"support_points": support_points, "data_points": data_points, "data_weight": data_weight}


def distances(block_points, data_points, data_norm):
    inner_part = jnp.dot(block_points, data_points.T, precision=lax.Precision.HIGHEST, preferred_element_type=jnp.float32)
    point_norm = jnp.sum(block_points * block_points, axis=1)
    return point_norm[:, None] + data_norm[None, :] - 2.0 * inner_part


def row_logsum(scores):
    peak = jnp.max(scores, axis=1)
    return peak + jnp.log(jnp.sum(jnp.exp(scores - peak[:, None]), axis=1))


def reference(support_points, data_points, data_weight):
    epsilon = D / 16.0
    log_support = -math.log(M)
    log_data = jnp.log(data_weight)
    data_norm = jnp.sum(data_points * data_points, axis=1)
    column_dual = jnp.zeros((N,), jnp.float32)
    points = support_points
    row_dual = jnp.zeros((M,), jnp.float32)
    for update_step in range(OUTER):
        blocked = points.reshape(N_SUPP, M_DEV, D)
        for inner_step in range(ITERS):
            def row_potential(block_points):
                dist = distances(block_points, data_points, data_norm)
                return epsilon * log_support - epsilon * row_logsum((column_dual[None, :] - dist) / epsilon)

            row_dual = lax.map(row_potential, blocked).reshape(M)
            dual_blocks = row_dual.reshape(N_SUPP, M_DEV)

            def column_step(running, inputs):
                col_peak, col_total = running
                block_points, block_dual = inputs
                scores = (block_dual[:, None] - distances(block_points, data_points, data_norm)) / epsilon
                new_peak = jnp.maximum(col_peak, jnp.max(scores, axis=0))
                col_total = col_total * jnp.exp(col_peak - new_peak) + jnp.sum(jnp.exp(scores - new_peak[None, :]), axis=0)
                return (new_peak, col_total), None

            start = (jnp.full((N,), -jnp.inf, jnp.float32), jnp.zeros((N,), jnp.float32))
            (col_peak, col_total), unused = lax.scan(column_step, start, (blocked, dual_blocks))
            column_dual = epsilon * log_data - epsilon * (col_peak + jnp.log(col_total))
        dual_blocks = row_dual.reshape(N_SUPP, M_DEV)

        def move_points(inputs):
            block_points, block_dual = inputs
            dist = distances(block_points, data_points, data_norm)
            transport = jnp.exp((block_dual[:, None] + column_dual[None, :] - dist) / epsilon)
            weighted = jnp.dot(transport, data_points, precision=lax.Precision.HIGHEST, preferred_element_type=jnp.float32)
            masses = jnp.sum(transport, axis=1)
            return weighted / masses[:, None]

        points = lax.map(move_points, (blocked, dual_blocks)).reshape(M, D)
    return points
```

```python
import math

import jax
import jax.numpy as jnp
from jax import lax
from jax.experimental import pallas as pl
from jax.experimental.pallas import tpu as pltpu
from jax.sharding import PartitionSpec as P

ITERS = 2
OUTER = 2
LANES = 128
ROWS = 64

F32 = jnp.float32
BF16 = jnp.bfloat16


def split(value):
    high = value.astype(BF16)
    low = (value - high.astype(F32)).astype(BF16)
    return high, low


def lane_row(block):
    return jnp.sum(block.T, axis=0, keepdims=True)


def spread_rows(vec_ref, out_ref):
    for a in range(vec_ref.shape[0]):
        block = jnp.broadcast_to(vec_ref[a : a + 1, :], (LANES, LANES))
        out_ref[a * LANES : (a + 1) * LANES, :] = block.T


def spread_cols(vec_ref, out_ref):
    for a in range(vec_ref.shape[0]):
        out_ref[:, a * LANES : (a + 1) * LANES] = jnp.broadcast_to(vec_ref[a : a + 1, :], (8, LANES))


def log_combine(parts):
    peak = jnp.max(parts, axis=0)
    return peak + jnp.log2(jnp.sum(jnp.exp2(parts - peak[None]), axis=0))


def tree(op, values):
    values = list(values)
    while len(values) > 1:
        values = [op(values[k], values[k + 1]) if k + 1 < len(values) else values[k] for k in range(0, len(values), 2)]
    return values[0]


def prepare_kernel(x_ref, high_ref, low_ref, norm_ref, *, scale):
    for a in range(x_ref.shape[0] // LANES):
        block = x_ref[a * LANES : (a + 1) * LANES, :]
        high, low = split(block)
        high_ref[a * LANES : (a + 1) * LANES, :] = high
        low_ref[a * LANES : (a + 1) * LANES, :] = low
        square = block * block
        folded = tree(jnp.add, [square[:, k : k + LANES] for k in range(0, block.shape[1], LANES)])
        norm_ref[a : a + 1, :] = lane_row(folded) * scale


def first_row_body(points_ref, high_ref, low_ref, shift_ref, scores_ref, norm_ref, out_ref, cols_ref, peak_ref, total_ref, scale):
    m, n = scores_ref.shape
    tiles = n // LANES
    high, low = split(points_ref[...] * (2.0 * scale))
    nt = (((1,), (1,)), ((), ()))
    for k in range(0, n, 256):
        xh = high_ref[k : k + 256, :]
        xl = low_ref[k : k + 256, :]
        acc = lax.dot_general(high, xh, nt, preferred_element_type=F32)
        acc = acc + lax.dot_general(high, xl, nt, preferred_element_type=F32)
        acc = acc + lax.dot_general(low, xh, nt, preferred_element_type=F32)
        scores_ref[:, k : k + 256] = acc
    spread_cols(shift_ref, cols_ref)

    def step(b, carry):
        for half in range(2):
            rows = pl.ds(pl.multiple_of(b * 16 + half * 8, 8), 8)
            q = [scores_ref[rows, t * LANES : (t + 1) * LANES] + cols_ref[:, t * LANES : (t + 1) * LANES] for t in range(tiles)]
            peak = tree(jnp.maximum, q)
            peak_ref[rows, :] = peak
            total_ref[rows, :] = tree(jnp.add, [jnp.exp2(v - peak) for v in q])
        return carry

    lax.fori_loop(0, m // 16, step, 0)
    for a in range(m // LANES):
        rows = slice(a * LANES, (a + 1) * LANES)
        block = points_ref[rows, :]
        square = block * block
        folded = tree(jnp.add, [square[:, k : k + LANES] for k in range(0, block.shape[1], LANES)])
        norm_ref[a : a + 1, :] = lane_row(folded) * scale
        peak = peak_ref[rows, :].T
        total = total_ref[rows, :].T
        top = jnp.max(peak, axis=0, keepdims=True)
        value = top + jnp.log2(jnp.sum(total * jnp.exp2(peak - top), axis=0, keepdims=True))
        for d in range(out_ref.shape[0]):
            out_ref[d, a : a + 1, :] = value


def first_row_kernel(points_ref, high_ref, low_ref, shift_ref, scores_ref, norm_ref, out_ref, cols_ref, peak_ref, total_ref, *, scale):
    first_row_body(points_ref, high_ref, low_ref, shift_ref, scores_ref, norm_ref, out_ref, cols_ref, peak_ref, total_ref, scale)


def next_row_kernel(core_ref, own_ref, other_ref, high_ref, low_ref, shift_ref, scores_ref, norm_ref, out_ref, cols_ref, peak_ref, total_ref, points_ref, *, scale):
    join(core_ref, own_ref, other_ref, points_ref)
    first_row_body(points_ref, high_ref, low_ref, shift_ref, scores_ref, norm_ref, out_ref, cols_ref, peak_ref, total_ref, scale)


def join(core_ref, own_ref, other_ref, points_ref):
    half = points_ref.shape[0] // 2
    core = core_ref[0]
    for d in range(own_ref.shape[0]):
        points_ref[pl.ds(pl.multiple_of(core * half + d * ROWS, ROWS), ROWS), :] = own_ref[d]
        points_ref[pl.ds(pl.multiple_of((1 - core) * half + d * ROWS, ROWS), ROWS), :] = other_ref[d]


def join_kernel(core_ref, own_ref, other_ref, points_ref):
    join(core_ref, own_ref, other_ref, points_ref)


def first_col_kernel(parts_ref, norm_ref, scores_ref, dual_ref, out_ref, rows_ref, *, log_support):
    m, n = scores_ref.shape
    norm = norm_ref[...]
    log_total = log_combine(parts_ref[...]) - norm
    dual_ref[...] = (log_support - log_total) - norm
    spread_rows(dual_ref, rows_ref)
    group = 4
    for t in range(0, n // LANES, group):
        cols = [slice((t + k) * LANES, (t + k + 1) * LANES) for k in range(group)]

        def top(b, peaks):
            peaks = list(peaks)
            for s in range(4):
                rows = pl.ds(pl.multiple_of(b * 32 + s * 8, 8), 8)
                f = rows_ref[rows, :]
                for k in range(group):
                    peaks[k] = jnp.maximum(peaks[k], scores_ref[rows, cols[k]] + f)
            return tuple(peaks)

        start = tuple(jnp.full((8, LANES), -jnp.inf, F32) for k in range(group))
        peaks = lax.fori_loop(0, m // 32, top, start)

        def add(b, totals):
            totals = list(totals)
            for s in range(4):
                rows = pl.ds(pl.multiple_of(b * 32 + s * 8, 8), 8)
                f = rows_ref[rows, :]
                for k in range(group):
                    totals[k] = totals[k] + jnp.exp2((scores_ref[rows, cols[k]] + f) - peaks[k])
            return tuple(totals)

        zero = tuple(jnp.zeros((8, LANES), F32) for k in range(group))
        totals = lax.fori_loop(0, m // 32, add, zero)
        for k in range(group):
            best = jnp.max(peaks[k], axis=0, keepdims=True)
            value = best + jnp.log2(jnp.sum(totals[k] * jnp.exp2(peaks[k] - best), axis=0, keepdims=True))
            for d in range(out_ref.shape[0]):
                out_ref[d, t + k : t + k + 1, :] = value


def next_row_sum_kernel(parts_ref, norm_ref, weight_ref, scores_ref, dual_ref, plan_ref, col_dual_ref, out_ref, shift_ref, cols_ref, rows_ref, total_ref):
    m, n = scores_ref.shape
    norm = norm_ref[...]
    col_dual = jnp.log2(weight_ref[...]) - (log_combine(parts_ref[...]) - norm)
    col_dual_ref[...] = col_dual
    shift_ref[...] = col_dual - norm
    spread_cols(shift_ref, cols_ref)
    spread_rows(dual_ref, rows_ref)

    def step(b, carry):
        for half in range(2):
            rows = pl.ds(pl.multiple_of(b * 16 + half * 8, 8), 8)
            f = rows_ref[rows, :]
            plan = []
            for t in range(n // LANES):
                cols = slice(t * LANES, (t + 1) * LANES)
                value = jnp.exp2((scores_ref[rows, cols] + f) + cols_ref[:, cols])
                plan_ref[rows, cols] = value
                plan.append(value)
            total_ref[rows, :] = tree(jnp.add, plan)
        return carry

    lax.fori_loop(0, m // 16, step, 0)
    for a in range(m // LANES):
        value = lane_row(total_ref[a * LANES : (a + 1) * LANES, :])
        for d in range(out_ref.shape[0]):
            out_ref[d, a : a + 1, :] = value


def next_col_sum_kernel(parts_ref, plan_ref, factor_ref, out_ref, rows_ref, *, share):
    m, n = plan_ref.shape
    factor_ref[...] = share / jnp.sum(parts_ref[...], axis=0)
    spread_rows(factor_ref, rows_ref)
    tiles = n // LANES

    def step(b, totals):
        totals = list(totals)
        for s in range(4):
            rows = pl.ds(pl.multiple_of(b * 32 + s * 8, 8), 8)
            u = rows_ref[rows, :]
            for t in range(tiles):
                totals[t] = totals[t] + plan_ref[rows, t * LANES : (t + 1) * LANES] * u
        return tuple(totals)

    totals = lax.fori_loop(0, m // 32, step, tuple(jnp.zeros((8, LANES), F32) for t in range(tiles)))
    for t in range(tiles):
        value = jnp.sum(totals[t], axis=0, keepdims=True)
        for d in range(out_ref.shape[0]):
            out_ref[d, t : t + 1, :] = value


def move_kernel(core_ref, parts_ref, weight_ref, col_dual_ref, norm_ref, factor_ref, plan_ref, high_ref, low_ref, keep_ref, send_ref, next_dual_ref, shift_ref, scale_ref, cols_ref, rows_ref, total_ref, acc_ref, left_ref, rest_ref):
    m, n = plan_ref.shape
    tiles = n // LANES
    scale_ref[...] = weight_ref[...] / jnp.sum(parts_ref[...], axis=0)
    next_dual = col_dual_ref[...] + jnp.log2(scale_ref[...])
    next_dual_ref[...] = next_dual
    shift_ref[...] = next_dual - norm_ref[...]
    spread_cols(scale_ref, cols_ref)
    spread_rows(factor_ref, rows_ref)

    def step(b, carry):
        rows = pl.ds(pl.multiple_of(b * 16, 16), 16)
        u = rows_ref[rows, :]
        plan = []
        for t in range(tiles):
            cols = slice(t * LANES, (t + 1) * LANES)
            v = cols_ref[:, cols]
            value = plan_ref[rows, cols] * u * jnp.concatenate([v, v], axis=0)
            high, low = split(value)
            left_ref[rows, cols] = high
            rest_ref[rows, cols] = low
            plan.append(value)
        total_ref[rows, :] = tree(jnp.add, plan)
        return carry

    lax.fori_loop(0, m // 16, step, 0)
    xh = high_ref[...]
    xl = low_ref[...]
    for a in range(0, m, 256):
        left = left_ref[a : a + 256, :]
        acc = jnp.dot(left, xh, preferred_element_type=F32)
        acc = acc + jnp.dot(left, xl, preferred_element_type=F32)
        acc = acc + jnp.dot(rest_ref[a : a + 256, :], xh, preferred_element_type=F32)
        acc_ref[a : a + 256, :] = acc
    half = m // 2
    core = core_ref[0]
    for a in range(m // LANES):
        scale_ref[a : a + 1, :] = lane_row(total_ref[a * LANES : (a + 1) * LANES, :])
    for part, out_ref in ((core, keep_ref), (1 - core, send_ref)):
        for d in range(out_ref.shape[0]):
            out_ref[d, :ROWS, :] = acc_ref[pl.ds(pl.multiple_of(part * half + d * ROWS, ROWS), ROWS), :]
            mass = scale_ref[pl.ds(part * (half // LANES) + d // 2, 1), :]
            out_ref[d, ROWS:, :LANES] = jnp.broadcast_to(mass, (8, LANES))
            out_ref[d, ROWS:, LANES:] = jnp.zeros((8, out_ref.shape[2] - LANES), F32)


def add_kernel(a_ref, b_ref, out_ref):
    out_ref[...] = a_ref[...] + b_ref[...]


def divide_kernel(place_ref, parts_ref, out_ref, mass_ref):
    parts = tree(jnp.add, [parts_ref[d] for d in range(parts_ref.shape[0])])
    mass_ref[...] = jnp.broadcast_to(parts[ROWS : ROWS + 1, :LANES], (LANES, LANES)).T
    mass = mass_ref[pl.ds(pl.multiple_of((place_ref[0] % 2) * ROWS, ROWS), ROWS), :]
    width = parts.shape[1]
    points = parts[:ROWS, :] / jnp.concatenate([mass] * (width // LANES), axis=1)
    for d in range(out_ref.shape[0]):
        out_ref[d] = points


def call(kernel, outs, scratch, name, smem=0, **params):
    vmem = pl.BlockSpec(memory_space=pltpu.VMEM)

    def run(*args):
        specs = [pl.BlockSpec(memory_space=pltpu.SMEM)] * smem + [vmem] * (len(args) - smem)
        return pl.pallas_call(
            (lambda *refs: kernel(*refs, **params)),
            out_shape=outs,
            in_specs=specs,
            out_specs=jax.tree.map(lambda o: vmem, outs),
            scratch_shapes=scratch,
            name=name,
            compiler_params=pltpu.CompilerParams(vmem_limit_bytes=48 * 1024 * 1024),
        )(*args)

    return run


def body(support_points, data_points, data_weight):
    m, dim = support_points.shape
    n = data_points.shape[0]
    dp = lax.axis_size("dp")
    supp = lax.axis_size("supp")
    epsilon = dim / 16.0
    scale = math.log2(math.e) / epsilon
    total = m * supp
    place = lax.axis_index("dp")
    core = (place % 2).astype(jnp.int32).reshape(1)
    chip = (place // 2).astype(jnp.int32).reshape(1)
    chips = dp // 2
    pairs = [(k, k ^ 1) for k in range(dp)]
    groups = [[2 * k + c for k in range(chips)] for c in range(2)]
    mr, nr = m // LANES, n // LANES
    sds = jax.ShapeDtypeStruct
    scores_t = sds((m, n), F32)
    row_t, col_t = sds((mr, LANES), F32), sds((nr, LANES), F32)
    row_parts_t, col_parts_t = sds((dp, mr, LANES), F32), sds((supp, nr, LANES), F32)
    wide_t = sds((chips, ROWS + 8, dim), F32)
    points_t = sds((chips, ROWS, dim), F32)
    row_s, col_s = pltpu.VMEM((m, LANES), F32), pltpu.VMEM((8, n), F32)

    def over_dp(parts):
        return lax.all_to_all(parts, "dp", 0, 0)

    def over_supp(parts):
        return lax.all_to_all(parts, "supp", 0, 0)

    weight = data_weight.reshape(nr, LANES)
    high, low, col_norm = call(prepare_kernel, (sds((n, dim), BF16), sds((n, dim), BF16), col_t), [], "prepare", scale=scale)(data_points)
    shift = -col_norm
    for update_step in range(OUTER):
        outs = (scores_t, row_t, row_parts_t)
        scratch = [col_s, row_s, row_s]
        if update_step == 0:
            scores, row_norm, parts = call(first_row_kernel, outs, scratch, "row0", scale=scale)(support_points, high, low, shift)
        else:
            scratch = scratch + [pltpu.VMEM((m, dim), F32)]
            scores, row_norm, parts = call(next_row_kernel, outs, scratch, "row1", smem=1, scale=scale)(core, own, other, high, low, shift)
        parts = over_dp(parts)
        row_dual, parts = call(first_col_kernel, (row_t, col_parts_t), [row_s], "col", log_support=-math.log2(total))(parts, row_norm, scores)
        parts = over_supp(parts)
        plan, col_dual, parts = call(next_row_sum_kernel, (scores_t, col_t, row_parts_t), [pltpu.VMEM((nr, LANES), F32), col_s, row_s, row_s], "plan")(parts, col_norm, weight, scores, row_dual)
        parts = over_dp(parts)
        factor, parts = call(next_col_sum_kernel, (row_t, col_parts_t), [row_s], "colsum", share=1.0 / total)(parts, plan)
        parts = over_supp(parts)
        scratch = [pltpu.VMEM((nr, LANES), F32), col_s, row_s, row_s, pltpu.VMEM((m, dim), F32), pltpu.VMEM((m, n), BF16), pltpu.VMEM((m, n), BF16)]
        keep, send, col_dual, shift = call(move_kernel, (wide_t, wide_t, col_t, col_t), scratch, "move", smem=1)(core, parts, weight, col_dual, col_norm, factor, plan, high, low)
        got = lax.ppermute(send, "dp", pairs)
        wide = call(add_kernel, wide_t, [], "add")(keep, got)
        wide = lax.all_to_all(wide, "dp", 0, 0, axis_index_groups=groups)
        own = call(divide_kernel, points_t, [pltpu.VMEM((LANES, LANES), F32)], "divide", smem=1)(chip, wide)
        own = lax.all_to_all(own, "dp", 0, 0, axis_index_groups=groups)
        other = lax.ppermute(own, "dp", pairs)
    return call(join_kernel, sds((m, dim), F32), [], "join", smem=1)(core, own, other)


def solution(mesh):
    return jax.shard_map(
        body,
        mesh=mesh,
        in_specs=(P("supp", None), P("dp", None), P("dp")),
        out_specs=P("supp", None),
        check_vma=False,
    )
```

```python
import math

import jax
import jax.numpy as jnp
from jax import lax
from jax.experimental import pallas as pl
from jax.experimental.pallas import tpu as pltpu
from jax.sharding import PartitionSpec as P

ITERS = 2
OUTER = 2
LANES = 128
ROWS = 64

F32 = jnp.float32
BF16 = jnp.bfloat16


def split(value):
    high = value.astype(BF16)
    low = (value - high.astype(F32)).astype(BF16)
    return high, low


def lane_row(block):
    return jnp.sum(block.T, axis=0, keepdims=True)


def spread_rows(vec_ref, out_ref):
    for a in range(vec_ref.shape[0]):
        block = jnp.broadcast_to(vec_ref[a : a + 1, :], (LANES, LANES))
        out_ref[a * LANES : (a + 1) * LANES, :] = block.T


def spread_cols(vec_ref, out_ref):
    for a in range(vec_ref.shape[0]):
        out_ref[:, a * LANES : (a + 1) * LANES] = jnp.broadcast_to(vec_ref[a : a + 1, :], (8, LANES))


def log_combine(parts):
    peak = jnp.max(parts, axis=0)
    return peak + jnp.log2(jnp.sum(jnp.exp2(parts - peak[None]), axis=0))


def tree(op, values):
    values = list(values)
    while len(values) > 1:
        values = [op(values[k], values[k + 1]) if k + 1 < len(values) else values[k] for k in range(0, len(values), 2)]
    return values[0]


def prepare_kernel(x_ref, high_ref, low_ref, norm_ref, *, scale):
    for a in range(x_ref.shape[0] // LANES):
        block = x_ref[a * LANES : (a + 1) * LANES, :]
        high, low = split(block)
        high_ref[a * LANES : (a + 1) * LANES, :] = high
        low_ref[a * LANES : (a + 1) * LANES, :] = low
        square = block * block
        folded = tree(jnp.add, [square[:, k : k + LANES] for k in range(0, block.shape[1], LANES)])
        norm_ref[a : a + 1, :] = lane_row(folded) * scale


def first_row_body(points_ref, high_ref, low_ref, shift_ref, scores_ref, norm_ref, out_ref, cols_ref, peak_ref, total_ref, scale):
    m, n = scores_ref.shape
    tiles = n // LANES
    high, low = split(points_ref[...] * (2.0 * scale))
    nt = (((1,), (1,)), ((), ()))
    for k in range(0, n, 256):
        xh = high_ref[k : k + 256, :]
        xl = low_ref[k : k + 256, :]
        acc = lax.dot_general(high, xh, nt, preferred_element_type=F32)
        acc = acc + lax.dot_general(high, xl, nt, preferred_element_type=F32)
        acc = acc + lax.dot_general(low, xh, nt, preferred_element_type=F32)
        scores_ref[:, k : k + 256] = acc
    spread_cols(shift_ref, cols_ref)

    def step(b, carry):
        for half in range(2):
            rows = pl.ds(pl.multiple_of(b * 16 + half * 8, 8), 8)
            q = [scores_ref[rows, t * LANES : (t + 1) * LANES] + cols_ref[:, t * LANES : (t + 1) * LANES] for t in range(tiles)]
            peak = tree(jnp.maximum, q)
            peak_ref[rows, :] = peak
            total_ref[rows, :] = tree(jnp.add, [jnp.exp2(v - peak) for v in q])
        return carry

    lax.fori_loop(0, m // 16, step, 0)
    for a in range(m // LANES):
        rows = slice(a * LANES, (a + 1) * LANES)
        block = points_ref[rows, :]
        square = block * block
        folded = tree(jnp.add, [square[:, k : k + LANES] for k in range(0, block.shape[1], LANES)])
        norm_ref[a : a + 1, :] = lane_row(folded) * scale
        peak = peak_ref[rows, :].T
        total = total_ref[rows, :].T
        top = jnp.max(peak, axis=0, keepdims=True)
        value = top + jnp.log2(jnp.sum(total * jnp.exp2(peak - top), axis=0, keepdims=True))
        for d in range(out_ref.shape[0]):
            out_ref[d, a : a + 1, :] = value


def first_row_kernel(points_ref, high_ref, low_ref, shift_ref, scores_ref, norm_ref, out_ref, cols_ref, peak_ref, total_ref, *, scale):
    first_row_body(points_ref, high_ref, low_ref, shift_ref, scores_ref, norm_ref, out_ref, cols_ref, peak_ref, total_ref, scale)


def next_row_kernel(core_ref, own_ref, other_ref, high_ref, low_ref, shift_ref, scores_ref, norm_ref, out_ref, cols_ref, peak_ref, total_ref, points_ref, *, scale):
    join(core_ref, own_ref, other_ref, points_ref)
    first_row_body(points_ref, high_ref, low_ref, shift_ref, scores_ref, norm_ref, out_ref, cols_ref, peak_ref, total_ref, scale)


def join(core_ref, own_ref, other_ref, points_ref):
    half = points_ref.shape[0] // 2
    core = core_ref[0]
    for d in range(own_ref.shape[0]):
        points_ref[pl.ds(pl.multiple_of(core * half + d * ROWS, ROWS), ROWS), :] = own_ref[d]
        points_ref[pl.ds(pl.multiple_of((1 - core) * half + d * ROWS, ROWS), ROWS), :] = other_ref[d]


def join_kernel(core_ref, own_ref, other_ref, points_ref):
    join(core_ref, own_ref, other_ref, points_ref)


def first_col_kernel(parts_ref, norm_ref, scores_ref, dual_ref, out_ref, rows_ref, *, log_support):
    m, n = scores_ref.shape
    norm = norm_ref[...]
    log_total = log_combine(parts_ref[...]) - norm
    dual_ref[...] = (log_support - log_total) - norm
    spread_rows(dual_ref, rows_ref)
    group = 4
    for t in range(0, n // LANES, group):
        cols = [slice((t + k) * LANES, (t + k + 1) * LANES) for k in range(group)]

        def top(b, peaks):
            peaks = list(peaks)
            for s in range(4):
                rows = pl.ds(pl.multiple_of(b * 32 + s * 8, 8), 8)
                f = rows_ref[rows, :]
                for k in range(group):
                    peaks[k] = jnp.maximum(peaks[k], scores_ref[rows, cols[k]] + f)
            return tuple(peaks)

        start = tuple(jnp.full((8, LANES), -jnp.inf, F32) for k in range(group))
        peaks = lax.fori_loop(0, m // 32, top, start)

        def add(b, totals):
            totals = list(totals)
            for s in range(4):
                rows = pl.ds(pl.multiple_of(b * 32 + s * 8, 8), 8)
                f = rows_ref[rows, :]
                for k in range(group):
                    totals[k] = totals[k] + jnp.exp2((scores_ref[rows, cols[k]] + f) - peaks[k])
            return tuple(totals)

        zero = tuple(jnp.zeros((8, LANES), F32) for k in range(group))
        totals = lax.fori_loop(0, m // 32, add, zero)
        for k in range(group):
            best = jnp.max(peaks[k], axis=0, keepdims=True)
            value = best + jnp.log2(jnp.sum(totals[k] * jnp.exp2(peaks[k] - best), axis=0, keepdims=True))
            for d in range(out_ref.shape[0]):
                out_ref[d, t + k : t + k + 1, :] = value


def next_row_sum_kernel(parts_ref, norm_ref, weight_ref, scores_ref, dual_ref, plan_ref, col_dual_ref, out_ref, shift_ref, cols_ref, rows_ref, total_ref):
    m, n = scores_ref.shape
    norm = norm_ref[...]
    col_dual = jnp.log2(weight_ref[...]) - (log_combine(parts_ref[...]) - norm)
    col_dual_ref[...] = col_dual
    shift_ref[...] = col_dual - norm
    spread_cols(shift_ref, cols_ref)
    spread_rows(dual_ref, rows_ref)

    def step(b, carry):
        for half in range(2):
            rows = pl.ds(pl.multiple_of(b * 16 + half * 8, 8), 8)
            f = rows_ref[rows, :]
            plan = []
            for t in range(n // LANES):
                cols = slice(t * LANES, (t + 1) * LANES)
                value = jnp.exp2((scores_ref[rows, cols] + f) + cols_ref[:, cols])
                plan_ref[rows, cols] = value
                plan.append(value)
            total_ref[rows, :] = tree(jnp.add, plan)
        return carry

    lax.fori_loop(0, m // 16, step, 0)
    for a in range(m // LANES):
        value = lane_row(total_ref[a * LANES : (a + 1) * LANES, :])
        for d in range(out_ref.shape[0]):
            out_ref[d, a : a + 1, :] = value


def next_col_sum_kernel(parts_ref, plan_ref, factor_ref, out_ref, rows_ref, *, share):
    m, n = plan_ref.shape
    factor_ref[...] = share / jnp.sum(parts_ref[...], axis=0)
    spread_rows(factor_ref, rows_ref)
    tiles = n // LANES

    def step(b, totals):
        totals = list(totals)
        for s in range(4):
            rows = pl.ds(pl.multiple_of(b * 32 + s * 8, 8), 8)
            u = rows_ref[rows, :]
            for t in range(tiles):
                totals[t] = totals[t] + plan_ref[rows, t * LANES : (t + 1) * LANES] * u
        return tuple(totals)

    totals = lax.fori_loop(0, m // 32, step, tuple(jnp.zeros((8, LANES), F32) for t in range(tiles)))
    for t in range(tiles):
        value = jnp.sum(totals[t], axis=0, keepdims=True)
        for d in range(out_ref.shape[0]):
            out_ref[d, t : t + 1, :] = value


def move_kernel(core_ref, parts_ref, weight_ref, col_dual_ref, norm_ref, factor_ref, plan_ref, high_ref, low_ref, keep_ref, send_ref, next_dual_ref, shift_ref, scale_ref, cols_ref, rows_ref, total_ref, acc_ref, left_ref, rest_ref):
    m, n = plan_ref.shape
    tiles = n // LANES
    scale_ref[...] = weight_ref[...] / jnp.sum(parts_ref[...], axis=0)
    next_dual = col_dual_ref[...] + jnp.log2(scale_ref[...])
    next_dual_ref[...] = next_dual
    shift_ref[...] = next_dual - norm_ref[...]
    spread_cols(scale_ref, cols_ref)
    spread_rows(factor_ref, rows_ref)

    def step(b, carry):
        rows = pl.ds(pl.multiple_of(b * 16, 16), 16)
        u = rows_ref[rows, :]
        plan = []
        for t in range(tiles):
            cols = slice(t * LANES, (t + 1) * LANES)
            v = cols_ref[:, cols]
            value = plan_ref[rows, cols] * u * jnp.concatenate([v, v], axis=0)
            high, low = split(value)
            left_ref[rows, cols] = high
            rest_ref[rows, cols] = low
            plan.append(value)
        total_ref[rows, :] = tree(jnp.add, plan)
        return carry

    lax.fori_loop(0, m // 16, step, 0)
    xh = high_ref[...]
    xl = low_ref[...]
    for a in range(0, m, 256):
        left = left_ref[a : a + 256, :]
        acc = jnp.dot(left, xh, preferred_element_type=F32)
        acc = acc + jnp.dot(left, xl, preferred_element_type=F32)
        acc = acc + jnp.dot(rest_ref[a : a + 256, :], xh, preferred_element_type=F32)
        acc_ref[a : a + 256, :] = acc
    half = m // 2
    core = core_ref[0]
    for a in range(m // LANES):
        scale_ref[a : a + 1, :] = lane_row(total_ref[a * LANES : (a + 1) * LANES, :])
    for part, out_ref in ((core, keep_ref), (1 - core, send_ref)):
        for d in range(out_ref.shape[0]):
            out_ref[d, :ROWS, :] = acc_ref[pl.ds(pl.multiple_of(part * half + d * ROWS, ROWS), ROWS), :]
            mass = scale_ref[pl.ds(part * (half // LANES) + d // 2, 1), :]
            out_ref[d, ROWS:, :LANES] = jnp.broadcast_to(mass, (8, LANES))
            out_ref[d, ROWS:, LANES:] = jnp.zeros((8, out_ref.shape[2] - LANES), F32)


def add_kernel(a_ref, b_ref, out_ref):
    out_ref[...] = a_ref[...] + b_ref[...]


def divide_kernel(place_ref, parts_ref, out_ref, mass_ref):
    parts = tree(jnp.add, [parts_ref[d] for d in range(parts_ref.shape[0])])
    mass_ref[...] = jnp.broadcast_to(parts[ROWS : ROWS + 1, :LANES], (LANES, LANES)).T
    mass = mass_ref[pl.ds(pl.multiple_of((place_ref[0] % 2) * ROWS, ROWS), ROWS), :]
    width = parts.shape[1]
    points = parts[:ROWS, :] / jnp.concatenate([mass] * (width // LANES), axis=1)
    for d in range(out_ref.shape[0]):
        out_ref[d] = points


def call(kernel, outs, scratch, name, smem=0, **params):
    vmem = pl.BlockSpec(memory_space=pltpu.VMEM)

    def run(*args):
        specs = [pl.BlockSpec(memory_space=pltpu.SMEM)] * smem + [vmem] * (len(args) - smem)
        return pl.pallas_call(
            (lambda *refs: kernel(*refs, **params)),
            out_shape=outs,
            in_specs=specs,
            out_specs=jax.tree.map(lambda o: vmem, outs),
            scratch_shapes=scratch,
            name=name,
            compiler_params=pltpu.CompilerParams(vmem_limit_bytes=24 * 1024 * 1024),
        )(*args)

    return run


def body(support_points, data_points, data_weight):
    m, dim = support_points.shape
    n = data_points.shape[0]
    dp = lax.axis_size("dp")
    supp = lax.axis_size("supp")
    epsilon = dim / 16.0
    scale = math.log2(math.e) / epsilon
    total = m * supp
    place = lax.axis_index("dp")
    core = (place % 2).astype(jnp.int32).reshape(1)
    chip = (place // 2).astype(jnp.int32).reshape(1)
    chips = dp // 2
    pairs = [(k, k ^ 1) for k in range(dp)]
    groups = [[2 * k + c for k in range(chips)] for c in range(2)]
    mr, nr = m // LANES, n // LANES
    sds = jax.ShapeDtypeStruct
    scores_t = sds((m, n), F32)
    row_t, col_t = sds((mr, LANES), F32), sds((nr, LANES), F32)
    row_parts_t, col_parts_t = sds((dp, mr, LANES), F32), sds((supp, nr, LANES), F32)
    wide_t = sds((chips, ROWS + 8, dim), F32)
    points_t = sds((chips, ROWS, dim), F32)
    row_s, col_s = pltpu.VMEM((m, LANES), F32), pltpu.VMEM((8, n), F32)

    def over_dp(parts):
        return lax.all_to_all(parts, "dp", 0, 0)

    def over_supp(parts):
        return lax.all_to_all(parts, "supp", 0, 0)

    weight = data_weight.reshape(nr, LANES)
    high, low, col_norm = call(prepare_kernel, (sds((n, dim), BF16), sds((n, dim), BF16), col_t), [], "prepare", scale=scale)(data_points)
    shift = -col_norm
    for update_step in range(OUTER):
        outs = (scores_t, row_t, row_parts_t)
        scratch = [col_s, row_s, row_s]
        if update_step == 0:
            scores, row_norm, parts = call(first_row_kernel, outs, scratch, "row0", scale=scale)(support_points, high, low, shift)
        else:
            scratch = scratch + [pltpu.VMEM((m, dim), F32)]
            scores, row_norm, parts = call(next_row_kernel, outs, scratch, "row1", smem=1, scale=scale)(core, own, other, high, low, shift)
        parts = over_dp(parts)
        row_dual, parts = call(first_col_kernel, (row_t, col_parts_t), [row_s], "col", log_support=-math.log2(total))(parts, row_norm, scores)
        parts = over_supp(parts)
        plan, col_dual, parts = call(next_row_sum_kernel, (scores_t, col_t, row_parts_t), [pltpu.VMEM((nr, LANES), F32), col_s, row_s, row_s], "plan")(parts, col_norm, weight, scores, row_dual)
        parts = over_dp(parts)
        factor, parts = call(next_col_sum_kernel, (row_t, col_parts_t), [row_s], "colsum", share=1.0 / total)(parts, plan)
        parts = over_supp(parts)
        scratch = [pltpu.VMEM((nr, LANES), F32), col_s, row_s, row_s, pltpu.VMEM((m, dim), F32), pltpu.VMEM((m, n), BF16), pltpu.VMEM((m, n), BF16)]
        keep, send, col_dual, shift = call(move_kernel, (wide_t, wide_t, col_t, col_t), scratch, "move", smem=1)(core, parts, weight, col_dual, col_norm, factor, plan, high, low)
        got = lax.ppermute(send, "dp", pairs)
        wide = call(add_kernel, wide_t, [], "add")(keep, got)
        wide = lax.all_to_all(wide, "dp", 0, 0, axis_index_groups=groups)
        own = call(divide_kernel, points_t, [pltpu.VMEM((LANES, LANES), F32)], "divide", smem=1)(chip, wide)
        own = lax.all_to_all(own, "dp", 0, 0, axis_index_groups=groups)
        other = lax.ppermute(own, "dp", pairs)
    return call(join_kernel, sds((m, dim), F32), [], "join", smem=1)(core, own, other)


def solution(mesh):
    return jax.shard_map(
        body,
        mesh=mesh,
        in_specs=(P("supp", None), P("dp", None), P("dp")),
        out_specs=P("supp", None),
        check_vma=False,
    )
```

```python
import math

import jax
import jax.numpy as jnp
from jax import lax
from jax.experimental import pallas as pl
from jax.experimental.pallas import tpu as pltpu
from jax.sharding import PartitionSpec as P

ITERS = 2
OUTER = 2
LANES = 128
ROWS = 64

F32 = jnp.float32
BF16 = jnp.bfloat16


def split(value):
    high = value.astype(BF16)
    low = (value - high.astype(F32)).astype(BF16)
    return high, low


def lane_row(block):
    return jnp.sum(block.T, axis=0, keepdims=True)


def spread_rows(vec_ref, out_ref):
    for a in range(vec_ref.shape[0]):
        block = jnp.broadcast_to(vec_ref[a : a + 1, :], (LANES, LANES))
        out_ref[a * LANES : (a + 1) * LANES, :] = block.T


def spread_cols(vec_ref, out_ref):
    for a in range(vec_ref.shape[0]):
        out_ref[:, a * LANES : (a + 1) * LANES] = jnp.broadcast_to(vec_ref[a : a + 1, :], (8, LANES))


def log_combine(parts):
    peak = jnp.max(parts, axis=0)
    return peak + jnp.log2(jnp.sum(jnp.exp2(parts - peak[None]), axis=0))


def tree(op, values):
    values = list(values)
    while len(values) > 1:
        values = [op(values[k], values[k + 1]) if k + 1 < len(values) else values[k] for k in range(0, len(values), 2)]
    return values[0]


def fold(block):
    return tree(jnp.add, [block[:, k : k + LANES] for k in range(0, block.shape[1], LANES)])


def prepare(x_ref, wide_ref, norm_ref, scale):
    dim = x_ref.shape[1]
    for a in range(x_ref.shape[0] // LANES):
        rows = slice(a * LANES, (a + 1) * LANES)
        block = x_ref[rows, :]
        high, low = split(block)
        wide_ref[rows, :dim] = high
        wide_ref[rows, dim : 2 * dim] = high
        wide_ref[rows, 2 * dim :] = low
        norm_ref[a : a + 1, :] = lane_row(fold(block * block)) * scale


def row_step(points_ref, wide_ref, shift_ref, scores_ref, plan_ref, norm_ref, top_ref, out_ref, cols_ref, peak_ref, total_ref, scale):
    m, n = scores_ref.shape
    tiles = n // LANES
    spread_cols(shift_ref, cols_ref)
    high, low = split(points_ref[...] * (2.0 * scale))
    left = jnp.concatenate([high, low, high], axis=1)
    for k in range(0, n, 256):
        acc = lax.dot_general(left, wide_ref[k : k + 256, :], (((1,), (1,)), ((), ())), preferred_element_type=F32)
        acc = acc + cols_ref[0:1, k : k + 256]
        scores_ref[:, k : k + 256] = acc
        best = jnp.maximum(acc[:, :LANES], acc[:, LANES:])
        peak_ref[...] = best if k == 0 else jnp.maximum(peak_ref[...], best)
    for a in range(m // LANES):
        rows = slice(a * LANES, (a + 1) * LANES)
        top = jnp.max(peak_ref[rows, :].T, axis=0, keepdims=True)
        top_ref[a : a + 1, :] = top
        peak_ref[rows, :] = jnp.broadcast_to(top, (LANES, LANES)).T

    def step(b, carry):
        for half in range(4):
            rows = pl.ds(pl.multiple_of(b * 32 + half * 8, 8), 8)
            peak = peak_ref[rows, :]
            values = []
            for t in range(tiles):
                cols = slice(t * LANES, (t + 1) * LANES)
                value = jnp.exp2(scores_ref[rows, cols] - peak)
                plan_ref[rows, cols] = value
                values.append(value)
            total_ref[rows, :] = tree(jnp.add, values)
        return carry

    lax.fori_loop(0, m // 32, step, 0)
    for a in range(m // LANES):
        rows = slice(a * LANES, (a + 1) * LANES)
        block = points_ref[rows, :]
        norm_ref[a : a + 1, :] = lane_row(fold(block * block)) * scale
        value = top_ref[a : a + 1, :] + jnp.log2(lane_row(total_ref[rows, :]))
        for d in range(out_ref.shape[0]):
            out_ref[d, a : a + 1, :] = value


def start_kernel(points_ref, x_ref, scores_ref, plan_ref, norm_ref, top_ref, out_ref, wide_ref, col_norm_ref, shift_ref, cols_ref, peak_ref, total_ref, *, scale):
    prepare(x_ref, wide_ref, col_norm_ref, scale)
    shift_ref[...] = -col_norm_ref[...]
    row_step(points_ref, wide_ref, shift_ref, scores_ref, plan_ref, norm_ref, top_ref, out_ref, cols_ref, peak_ref, total_ref, scale)


def next_row_kernel(own_ref, other_ref, wide_ref, shift_ref, scores_ref, plan_ref, norm_ref, top_ref, out_ref, cols_ref, peak_ref, total_ref, points_ref, *, scale):
    join(own_ref, other_ref, points_ref)
    row_step(points_ref, wide_ref, shift_ref, scores_ref, plan_ref, norm_ref, top_ref, out_ref, cols_ref, peak_ref, total_ref, scale)


def core_index():
    return lax.axis_index("dp") % 2


def join(own_ref, other_ref, points_ref):
    half = points_ref.shape[0] // 2
    core = core_index()
    for d in range(own_ref.shape[0]):
        points_ref[pl.ds(pl.multiple_of(core * half + d * ROWS, ROWS), ROWS), :] = own_ref[d]
        points_ref[pl.ds(pl.multiple_of((1 - core) * half + d * ROWS, ROWS), ROWS), :] = other_ref[d]


def join_kernel(own_ref, other_ref, points_ref):
    join(own_ref, other_ref, points_ref)


def column_sums(plan_ref, rows_ref):
    m, n = plan_ref.shape
    tiles = n // LANES

    def step(b, totals):
        totals = list(totals)
        for s in range(4):
            rows = pl.ds(pl.multiple_of(b * 32 + s * 8, 8), 8)
            u = rows_ref[rows, :]
            for t in range(tiles):
                totals[t] = totals[t] + plan_ref[rows, t * LANES : (t + 1) * LANES] * u
        return tuple(totals)

    totals = lax.fori_loop(0, m // 32, step, tuple(jnp.zeros((8, LANES), F32) for t in range(tiles)))
    return [jnp.sum(total, axis=0, keepdims=True) for total in totals]


def first_col_kernel(parts_ref, norm_ref, top_ref, shift_ref, scores_ref, plan_ref, dual_ref, out_ref, rows_ref, factor_ref, *, log_support):
    m, n = scores_ref.shape
    norm = norm_ref[...]
    log_total = log_combine(parts_ref[...]) - norm
    dual = (log_support - log_total) - norm
    dual_ref[...] = dual
    factor_ref[...] = jnp.exp2(dual + top_ref[...])
    spread_rows(factor_ref, rows_ref)
    sums = column_sums(plan_ref, rows_ref)
    for t, value in enumerate(sums):
        value = jnp.log2(value) - shift_ref[t : t + 1, :]
        for d in range(out_ref.shape[0]):
            out_ref[d, t : t + 1, :] = value

    @pl.when(jnp.min(tree(jnp.minimum, sums)) < 2.0**-80)
    def _():
        spread_rows(dual_ref, rows_ref)
        for t in range(n // LANES):
            cols = slice(t * LANES, (t + 1) * LANES)

            def top(b, peak):
                rows = pl.ds(pl.multiple_of(b * 8, 8), 8)
                return jnp.maximum(peak, scores_ref[rows, cols] + rows_ref[rows, :])

            peak = lax.fori_loop(0, m // 8, top, jnp.full((8, LANES), -jnp.inf, F32), unroll=8)
            best = jnp.max(peak, axis=0, keepdims=True)

            def add(b, total):
                rows = pl.ds(pl.multiple_of(b * 8, 8), 8)
                return total + jnp.exp2((scores_ref[rows, cols] + rows_ref[rows, :]) - best)

            total = lax.fori_loop(0, m // 8, add, jnp.zeros((8, LANES), F32), unroll=8)
            value = best + jnp.log2(jnp.sum(total, axis=0, keepdims=True)) - shift_ref[t : t + 1, :]
            for d in range(out_ref.shape[0]):
                out_ref[d, t : t + 1, :] = value


def next_row_sum_kernel(parts_ref, norm_ref, weight_ref, shift_ref, scores_ref, dual_ref, plan_ref, col_dual_ref, out_ref, delta_ref, cols_ref, rows_ref, total_ref):
    m, n = scores_ref.shape
    norm = norm_ref[...]
    col_dual = jnp.log2(weight_ref[...]) - (log_combine(parts_ref[...]) - norm)
    col_dual_ref[...] = col_dual
    delta_ref[...] = (col_dual - norm) - shift_ref[...]
    spread_cols(delta_ref, cols_ref)
    spread_rows(dual_ref, rows_ref)

    def step(b, carry):
        for half in range(4):
            rows = pl.ds(pl.multiple_of(b * 32 + half * 8, 8), 8)
            f = rows_ref[rows, :]
            plan = []
            for t in range(n // LANES):
                cols = slice(t * LANES, (t + 1) * LANES)
                value = jnp.exp2((scores_ref[rows, cols] + f) + cols_ref[:, cols])
                plan_ref[rows, cols] = value
                plan.append(value)
            total_ref[rows, :] = tree(jnp.add, plan)
        return carry

    lax.fori_loop(0, m // 32, step, 0)
    for a in range(m // LANES):
        value = lane_row(total_ref[a * LANES : (a + 1) * LANES, :])
        for d in range(out_ref.shape[0]):
            out_ref[d, a : a + 1, :] = value


def next_col_sum_kernel(parts_ref, plan_ref, factor_ref, out_ref, rows_ref, *, share):
    factor_ref[...] = share / jnp.sum(parts_ref[...], axis=0)
    spread_rows(factor_ref, rows_ref)
    for t, value in enumerate(column_sums(plan_ref, rows_ref)):
        for d in range(out_ref.shape[0]):
            out_ref[d, t : t + 1, :] = value


def move_half(half, plan_ref, factor_ref, ratio_ref, high_ref, low_ref, out_ref, rows_ref, mass_ref, acc_ref):
    n = plan_ref.shape[1]
    rows_here = plan_ref.shape[0] // 2
    spread_rows(factor_ref, rows_ref)
    high = high_ref[...]
    low = low_ref[...]
    for b in range(rows_here // 256):
        at = pl.ds(pl.multiple_of(half * rows_here + b * 256, 256), 256)
        plan = plan_ref[at, :]
        left, rest = split(plan)
        acc = jnp.dot(left, high, preferred_element_type=F32)
        acc = acc + jnp.dot(left, low, preferred_element_type=F32)
        acc = acc + jnp.dot(rest, high, preferred_element_type=F32)
        u = rows_ref[at, :]
        acc_ref[b * 256 : (b + 1) * 256, :] = acc * jnp.concatenate([u] * (acc.shape[1] // LANES), axis=1)
        mass = tree(jnp.add, [plan[:, t * LANES : (t + 1) * LANES] * ratio_ref[t : t + 1, :] for t in range(n // LANES)])
        mass = mass * u
        for a in range(2):
            mass_ref[2 * b + a : 2 * b + a + 1, :] = lane_row(mass[a * LANES : (a + 1) * LANES, :])
    for d in range(out_ref.shape[0]):
        points = acc_ref[d * ROWS : (d + 1) * ROWS, :]
        mass = jnp.broadcast_to(mass_ref[d // 2 : d // 2 + 1, :], (8, LANES))
        out_ref[d, :ROWS, :] = points
        out_ref[d, ROWS:, :LANES] = mass
        out_ref[d, ROWS:, LANES:] = jnp.zeros((8, out_ref.shape[2] - LANES), F32)


def send_kernel(parts_ref, weight_ref, col_dual_ref, norm_ref, factor_ref, plan_ref, x_ref, send_ref, high_ref, low_ref, ratio_ref, shift_ref, rows_ref, mass_ref, acc_ref):
    ratio_ref[...] = weight_ref[...] / jnp.sum(parts_ref[...], axis=0)
    shift_ref[...] = (col_dual_ref[...] + jnp.log2(ratio_ref[...])) - norm_ref[...]
    for a in range(x_ref.shape[0] // LANES):
        rows = slice(a * LANES, (a + 1) * LANES)
        v = jnp.broadcast_to(ratio_ref[a : a + 1, :], (LANES, LANES)).T
        high, low = split(x_ref[rows, :] * jnp.concatenate([v] * (x_ref.shape[1] // LANES), axis=1))
        high_ref[rows, :] = high
        low_ref[rows, :] = low
    move_half(1 - core_index(), plan_ref, factor_ref, ratio_ref, high_ref, low_ref, send_ref, rows_ref, mass_ref, acc_ref)


def keep_kernel(ratio_ref, factor_ref, plan_ref, high_ref, low_ref, out_ref, rows_ref, mass_ref, acc_ref):
    move_half(core_index(), plan_ref, factor_ref, ratio_ref, high_ref, low_ref, out_ref, rows_ref, mass_ref, acc_ref)


def add_kernel(a_ref, b_ref, out_ref):
    out_ref[...] = a_ref[...] + b_ref[...]


def divide_kernel(parts_ref, out_ref, mass_ref):
    parts = tree(jnp.add, [parts_ref[d] for d in range(parts_ref.shape[0])])
    mass_ref[...] = jnp.broadcast_to(parts[ROWS : ROWS + 1, :LANES], (LANES, LANES)).T
    mass = mass_ref[pl.ds(pl.multiple_of((lax.axis_index("dp") // 2 % 2) * ROWS, ROWS), ROWS), :]
    width = parts.shape[1]
    points = parts[:ROWS, :] / jnp.concatenate([mass] * (width // LANES), axis=1)
    for d in range(out_ref.shape[0]):
        out_ref[d] = points


def call(kernel, outs, scratch, name, **params):
    vmem = pl.BlockSpec(memory_space=pltpu.VMEM)

    def run(*args):
        return pl.pallas_call(
            (lambda *refs: kernel(*refs, **params)),
            out_shape=outs,
            in_specs=[vmem] * len(args),
            out_specs=jax.tree.map(lambda o: vmem, outs),
            scratch_shapes=scratch,
            name=name,
            compiler_params=pltpu.CompilerParams(vmem_limit_bytes=20 * 1024 * 1024),
        )(*args)

    return run


def body(support_points, data_points, data_weight):
    m, dim = support_points.shape
    n = data_points.shape[0]
    dp = lax.axis_size("dp")
    supp = lax.axis_size("supp")
    epsilon = dim / 16.0
    scale = math.log2(math.e) / epsilon
    total = m * supp
    chips = dp // 2
    pairs = [(k, k ^ 1) for k in range(dp)]
    groups = [[2 * k + c for k in range(chips)] for c in range(2)]
    mr, nr = m // LANES, n // LANES
    sds = jax.ShapeDtypeStruct
    scores_t = sds((m, n), F32)
    row_t, col_t = sds((mr, LANES), F32), sds((nr, LANES), F32)
    row_parts_t, col_parts_t = sds((dp, mr, LANES), F32), sds((supp, nr, LANES), F32)
    wide_t = sds((chips, ROWS + 8, dim), F32)
    points_t = sds((chips, ROWS, dim), F32)
    row_s, col_s = pltpu.VMEM((m, LANES), F32), pltpu.VMEM((8, n), F32)

    def over_dp(parts):
        return lax.all_to_all(parts, "dp", 0, 0)

    def over_supp(parts):
        return lax.all_to_all(parts, "supp", 0, 0)

    weight = data_weight.reshape(nr, LANES)
    half_t = sds((n, dim), BF16)
    mass_s = pltpu.VMEM((8, LANES), F32)
    acc_s = pltpu.VMEM((m // 2, dim), F32)
    for update_step in range(OUTER):
        outs = (scores_t, scores_t, row_t, row_t, row_parts_t)
        scratch = [col_s, row_s, row_s]
        if update_step == 0:
            outs = outs + (sds((n, 3 * dim), BF16), col_t, col_t)
            scores, raw, row_norm, top, parts, wide_x, col_norm, shift = call(start_kernel, outs, scratch, "row0", scale=scale)(support_points, data_points)
        else:
            scratch = scratch + [pltpu.VMEM((m, dim), F32)]
            scores, raw, row_norm, top, parts = call(next_row_kernel, outs, scratch, "row1", scale=scale)(own, other, wide_x, shift)
        parts = over_dp(parts)
        row_dual, parts = call(first_col_kernel, (row_t, col_parts_t), [row_s, pltpu.VMEM((mr, LANES), F32)], "col", log_support=-math.log2(total))(parts, row_norm, top, shift, scores, raw)
        parts = over_supp(parts)
        plan, col_dual, parts = call(next_row_sum_kernel, (scores_t, col_t, row_parts_t), [pltpu.VMEM((nr, LANES), F32), col_s, row_s, row_s], "plan")(parts, col_norm, weight, shift, scores, row_dual)
        parts = over_dp(parts)
        factor, parts = call(next_col_sum_kernel, (row_t, col_parts_t), [row_s], "colsum", share=1.0 / total)(parts, plan)
        parts = over_supp(parts)
        send, high, low, ratio, shift = call(send_kernel, (wide_t, half_t, half_t, col_t, col_t), [row_s, mass_s, acc_s], "send")(parts, weight, col_dual, col_norm, factor, plan, data_points)
        got = lax.ppermute(send, "dp", pairs)
        wide = call(keep_kernel, wide_t, [row_s, mass_s, acc_s], "keep")(ratio, factor, plan, high, low)
        wide = call(add_kernel, wide_t, [], "add")(wide, got)
        wide = lax.all_to_all(wide, "dp", 0, 0, axis_index_groups=groups)
        own = call(divide_kernel, points_t, [pltpu.VMEM((LANES, LANES), F32)], "divide")(wide)
        own = lax.all_to_all(own, "dp", 0, 0, axis_index_groups=groups)
        other = lax.ppermute(own, "dp", pairs)
    return call(join_kernel, sds((m, dim), F32), [], "join")(own, other)


def solution(mesh):
    return jax.shard_map(
        body,
        mesh=mesh,
        in_specs=(P("supp", None), P("dp", None), P("dp")),
        out_specs=P("supp", None),
        check_vma=False,
    )
```

```python
import math

import jax
import jax.numpy as jnp
from jax import lax
from jax.experimental import pallas as pl
from jax.experimental.pallas import tpu as pltpu
from jax.sharding import PartitionSpec as P

ITERS = 2
OUTER = 2
LANES = 128
ROWS = 64

F32 = jnp.float32
BF16 = jnp.bfloat16


def split(value):
    high = value.astype(BF16)
    low = (value - high.astype(F32)).astype(BF16)
    return high, low


def lane_row(block):
    return jnp.sum(block.T, axis=0, keepdims=True)


def spread_rows(vec_ref, out_ref):
    for a in range(vec_ref.shape[0]):
        block = jnp.broadcast_to(vec_ref[a : a + 1, :], (LANES, LANES))
        out_ref[a * LANES : (a + 1) * LANES, :] = block.T


def spread_cols(vec_ref, out_ref):
    for a in range(vec_ref.shape[0]):
        out_ref[:, a * LANES : (a + 1) * LANES] = jnp.broadcast_to(vec_ref[a : a + 1, :], (8, LANES))


def log_combine(parts):
    peak = jnp.max(parts, axis=0)
    return peak + jnp.log2(jnp.sum(jnp.exp2(parts - peak[None]), axis=0))


def tree(op, values):
    values = list(values)
    while len(values) > 1:
        values = [op(values[k], values[k + 1]) if k + 1 < len(values) else values[k] for k in range(0, len(values), 2)]
    return values[0]


def fold(block):
    return tree(jnp.add, [block[:, k : k + LANES] for k in range(0, block.shape[1], LANES)])


def prepare(x_ref, wide_ref, norm_ref, scale, start, count):
    dim = x_ref.shape[1]
    for a in range(start // LANES, (start + count) // LANES):
        rows = slice(a * LANES, (a + 1) * LANES)
        block = x_ref[rows, :]
        high, low = split(block)
        wide_ref[rows, :dim] = high
        wide_ref[rows, dim : 2 * dim] = high
        wide_ref[rows, 2 * dim :] = low
        norm_ref[a : a + 1, :] = lane_row(fold(block * block)) * scale


def row_step(points_ref, wide_ref, shift_ref, scores_ref, plan_ref, norm_ref, top_ref, out_ref, cols_ref, peak_ref, total_ref, scale):
    m, n = scores_ref.shape
    tiles = n // LANES
    spread_cols(shift_ref, cols_ref)
    high, low = split(points_ref[...] * (2.0 * scale))
    left = jnp.concatenate([high, low, high], axis=1)
    for k in range(0, n, 256):
        acc = lax.dot_general(left, wide_ref[k : k + 256, :], (((1,), (1,)), ((), ())), preferred_element_type=F32)
        acc = acc + cols_ref[0:1, k : k + 256]
        scores_ref[:, k : k + 256] = acc
        best = jnp.maximum(acc[:, :LANES], acc[:, LANES:])
        peak_ref[...] = best if k == 0 else jnp.maximum(peak_ref[...], best)
    for a in range(m // LANES):
        rows = slice(a * LANES, (a + 1) * LANES)
        top = jnp.max(peak_ref[rows, :].T, axis=0, keepdims=True)
        top_ref[a : a + 1, :] = top
        peak_ref[rows, :] = jnp.broadcast_to(top, (LANES, LANES)).T

    def step(b, carry):
        for half in range(4):
            rows = pl.ds(pl.multiple_of(b * 32 + half * 8, 8), 8)
            peak = peak_ref[rows, :]
            values = []
            for t in range(tiles):
                cols = slice(t * LANES, (t + 1) * LANES)
                value = jnp.exp2(scores_ref[rows, cols] - peak)
                plan_ref[rows, cols] = value
                values.append(value)
            total_ref[rows, :] = tree(jnp.add, values)
        return carry

    lax.fori_loop(0, m // 32, step, 0)
    for a in range(m // LANES):
        rows = slice(a * LANES, (a + 1) * LANES)
        block = points_ref[rows, :]
        norm_ref[a : a + 1, :] = lane_row(fold(block * block)) * scale
        value = top_ref[a : a + 1, :] + jnp.log2(lane_row(total_ref[rows, :]))
        for d in range(out_ref.shape[0]):
            out_ref[d, a : a + 1, :] = value


def start_kernel(points_hbm, x_hbm, scores_ref, plan_ref, norm_ref, top_ref, out_ref, wide_ref, col_norm_ref, shift_ref, cols_ref, peak_ref, total_ref, points_ref, x_ref, sems, *, scale):
    pieces = 4
    count = x_ref.shape[0] // pieces
    copies = [pltpu.make_async_copy(x_hbm.at[k * count : (k + 1) * count], x_ref.at[k * count : (k + 1) * count], sems.at[k]) for k in range(pieces)]
    copies.append(pltpu.make_async_copy(points_hbm, points_ref, sems.at[pieces]))
    for copy in copies:
        copy.start()
    for k in range(pieces):
        copies[k].wait()
        prepare(x_ref, wide_ref, col_norm_ref, scale, k * count, count)
    copies[pieces].wait()
    shift_ref[...] = -col_norm_ref[...]
    row_step(points_ref, wide_ref, shift_ref, scores_ref, plan_ref, norm_ref, top_ref, out_ref, cols_ref, peak_ref, total_ref, scale)


def next_row_kernel(own_ref, other_ref, wide_ref, shift_ref, scores_ref, plan_ref, norm_ref, top_ref, out_ref, cols_ref, peak_ref, total_ref, points_ref, *, scale):
    join(own_ref, other_ref, points_ref)
    row_step(points_ref, wide_ref, shift_ref, scores_ref, plan_ref, norm_ref, top_ref, out_ref, cols_ref, peak_ref, total_ref, scale)


def core_index():
    return lax.axis_index("dp") % 2


def join(own_ref, other_ref, points_ref):
    half = points_ref.shape[0] // 2
    core = core_index()
    for d in range(own_ref.shape[0]):
        points_ref[pl.ds(pl.multiple_of(core * half + d * ROWS, ROWS), ROWS), :] = own_ref[d]
        points_ref[pl.ds(pl.multiple_of((1 - core) * half + d * ROWS, ROWS), ROWS), :] = other_ref[d]


def join_kernel(own_ref, other_ref, points_hbm, sems):
    half = own_ref.shape[0]
    core = core_index()
    first = pltpu.make_async_copy(own_ref, points_hbm.at[pl.ds(pl.multiple_of(core * half, half), half)], sems.at[0])
    second = pltpu.make_async_copy(other_ref, points_hbm.at[pl.ds(pl.multiple_of((1 - core) * half, half), half)], sems.at[1])
    first.start()
    second.start()
    first.wait()
    second.wait()


def column_sums(plan_ref, rows_ref):
    m, n = plan_ref.shape
    tiles = n // LANES

    def step(b, totals):
        totals = list(totals)
        for s in range(4):
            rows = pl.ds(pl.multiple_of(b * 32 + s * 8, 8), 8)
            u = rows_ref[rows, :]
            for t in range(tiles):
                totals[t] = totals[t] + plan_ref[rows, t * LANES : (t + 1) * LANES] * u
        return tuple(totals)

    totals = lax.fori_loop(0, m // 32, step, tuple(jnp.zeros((8, LANES), F32) for t in range(tiles)))
    return [jnp.sum(total, axis=0, keepdims=True) for total in totals]


def first_col_kernel(parts_ref, norm_ref, top_ref, shift_ref, scores_ref, plan_ref, dual_ref, out_ref, rows_ref, factor_ref, *, log_support):
    m, n = scores_ref.shape
    norm = norm_ref[...]
    log_total = log_combine(parts_ref[...]) - norm
    dual = (log_support - log_total) - norm
    dual_ref[...] = dual
    factor_ref[...] = jnp.exp2(dual + top_ref[...])
    spread_rows(factor_ref, rows_ref)
    sums = column_sums(plan_ref, rows_ref)
    for t, value in enumerate(sums):
        value = jnp.log2(value) - shift_ref[t : t + 1, :]
        for d in range(out_ref.shape[0]):
            out_ref[d, t : t + 1, :] = value

    @pl.when(jnp.min(tree(jnp.minimum, sums)) < 2.0**-80)
    def _():
        spread_rows(dual_ref, rows_ref)
        for t in range(n // LANES):
            cols = slice(t * LANES, (t + 1) * LANES)

            def top(b, peak):
                rows = pl.ds(pl.multiple_of(b * 8, 8), 8)
                return jnp.maximum(peak, scores_ref[rows, cols] + rows_ref[rows, :])

            peak = lax.fori_loop(0, m // 8, top, jnp.full((8, LANES), -jnp.inf, F32), unroll=8)
            best = jnp.max(peak, axis=0, keepdims=True)

            def add(b, total):
                rows = pl.ds(pl.multiple_of(b * 8, 8), 8)
                return total + jnp.exp2((scores_ref[rows, cols] + rows_ref[rows, :]) - best)

            total = lax.fori_loop(0, m // 8, add, jnp.zeros((8, LANES), F32), unroll=8)
            value = best + jnp.log2(jnp.sum(total, axis=0, keepdims=True)) - shift_ref[t : t + 1, :]
            for d in range(out_ref.shape[0]):
                out_ref[d, t : t + 1, :] = value


def next_row_sum_kernel(parts_ref, norm_ref, weight_ref, shift_ref, scores_ref, dual_ref, plan_ref, col_dual_ref, out_ref, delta_ref, cols_ref, rows_ref, total_ref):
    m, n = scores_ref.shape
    norm = norm_ref[...]
    col_dual = jnp.log2(weight_ref[...]) - (log_combine(parts_ref[...]) - norm)
    col_dual_ref[...] = col_dual
    delta_ref[...] = (col_dual - norm) - shift_ref[...]
    spread_cols(delta_ref, cols_ref)
    spread_rows(dual_ref, rows_ref)

    def step(b, carry):
        for half in range(4):
            rows = pl.ds(pl.multiple_of(b * 32 + half * 8, 8), 8)
            f = rows_ref[rows, :]
            plan = []
            for t in range(n // LANES):
                cols = slice(t * LANES, (t + 1) * LANES)
                value = jnp.exp2((scores_ref[rows, cols] + f) + cols_ref[:, cols])
                plan_ref[rows, cols] = value
                plan.append(value)
            total_ref[rows, :] = tree(jnp.add, plan)
        return carry

    lax.fori_loop(0, m // 32, step, 0)
    for a in range(m // LANES):
        value = lane_row(total_ref[a * LANES : (a + 1) * LANES, :])
        for d in range(out_ref.shape[0]):
            out_ref[d, a : a + 1, :] = value


def next_col_sum_kernel(parts_ref, plan_ref, factor_ref, out_ref, rows_ref, *, share):
    factor_ref[...] = share / jnp.sum(parts_ref[...], axis=0)
    spread_rows(factor_ref, rows_ref)
    for t, value in enumerate(column_sums(plan_ref, rows_ref)):
        for d in range(out_ref.shape[0]):
            out_ref[d, t : t + 1, :] = value


def move_half(half, plan_ref, factor_ref, ratio_ref, stack_ref, out_ref, rows_ref, mass_ref, acc_ref):
    n = plan_ref.shape[1]
    rows_here = plan_ref.shape[0] // 2
    spread_rows(factor_ref, rows_ref)
    stack = stack_ref[...]
    for b in range(rows_here // 256):
        at = pl.ds(pl.multiple_of(half * rows_here + b * 256, 256), 256)
        plan = plan_ref[at, :]
        left, rest = split(plan)
        acc = jnp.dot(jnp.concatenate([left, left, rest], axis=1), stack, preferred_element_type=F32)
        u = rows_ref[at, :]
        acc_ref[b * 256 : (b + 1) * 256, :] = acc * jnp.concatenate([u] * (acc.shape[1] // LANES), axis=1)
        mass = tree(jnp.add, [plan[:, t * LANES : (t + 1) * LANES] * ratio_ref[t : t + 1, :] for t in range(n // LANES)])
        mass = mass * u
        for a in range(2):
            mass_ref[2 * b + a : 2 * b + a + 1, :] = lane_row(mass[a * LANES : (a + 1) * LANES, :])
    tiles = acc_ref.shape[1] // LANES
    for d in range(out_ref.shape[0]):
        for t in range(tiles):
            out_ref[d, t * ROWS : (t + 1) * ROWS, :] = acc_ref[d * ROWS : (d + 1) * ROWS, t * LANES : (t + 1) * LANES]
        out_ref[d, tiles * ROWS :, :] = jnp.broadcast_to(mass_ref[d // 2 : d // 2 + 1, :], (8, LANES))


def send_kernel(parts_ref, weight_ref, col_dual_ref, norm_ref, factor_ref, plan_ref, x_ref, send_ref, stack_ref, ratio_ref, shift_ref, rows_ref, mass_ref, acc_ref):
    n = x_ref.shape[0]
    ratio_ref[...] = weight_ref[...] / jnp.sum(parts_ref[...], axis=0)
    shift_ref[...] = (col_dual_ref[...] + jnp.log2(ratio_ref[...])) - norm_ref[...]
    for a in range(0, n, LANES):
        v = jnp.broadcast_to(ratio_ref[a // LANES : a // LANES + 1, :], (LANES, LANES)).T
        high, low = split(x_ref[a : a + LANES, :] * jnp.concatenate([v] * (x_ref.shape[1] // LANES), axis=1))
        stack_ref[a : a + LANES, :] = high
        stack_ref[n + a : n + a + LANES, :] = low
        stack_ref[2 * n + a : 2 * n + a + LANES, :] = high
    move_half(1 - core_index(), plan_ref, factor_ref, ratio_ref, stack_ref, send_ref, rows_ref, mass_ref, acc_ref)


def keep_kernel(ratio_ref, factor_ref, plan_ref, stack_ref, out_ref, rows_ref, mass_ref, acc_ref):
    move_half(core_index(), plan_ref, factor_ref, ratio_ref, stack_ref, out_ref, rows_ref, mass_ref, acc_ref)


def add_kernel(a_ref, b_ref, out_ref):
    out_ref[...] = a_ref[...] + b_ref[...]


def divide_kernel(parts_ref, out_ref, mass_ref):
    parts = tree(jnp.add, [parts_ref[d] for d in range(parts_ref.shape[0])])
    tiles = out_ref.shape[2] // LANES
    mass_ref[...] = jnp.broadcast_to(parts[tiles * ROWS : tiles * ROWS + 1, :], (LANES, LANES)).T
    mass = mass_ref[pl.ds(pl.multiple_of((lax.axis_index("dp") // 2 % 2) * ROWS, ROWS), ROWS), :]
    points = jnp.concatenate([parts[t * ROWS : (t + 1) * ROWS, :] / mass for t in range(tiles)], axis=1)
    for d in range(out_ref.shape[0]):
        out_ref[d] = points


def call(kernel, outs, scratch, name, inputs=pltpu.VMEM, outputs=pltpu.VMEM, **params):
    def run(*args):
        return pl.pallas_call(
            (lambda *refs: kernel(*refs, **params)),
            out_shape=outs,
            in_specs=[pl.BlockSpec(memory_space=inputs)] * len(args),
            out_specs=jax.tree.map(lambda o: pl.BlockSpec(memory_space=outputs), outs),
            scratch_shapes=scratch,
            name=name,
            compiler_params=pltpu.CompilerParams(vmem_limit_bytes=20 * 1024 * 1024),
        )(*args)

    return run


def body(support_points, data_points, data_weight):
    m, dim = support_points.shape
    n = data_points.shape[0]
    dp = lax.axis_size("dp")
    supp = lax.axis_size("supp")
    epsilon = dim / 16.0
    scale = math.log2(math.e) / epsilon
    total = m * supp
    chips = dp // 2
    pairs = [(k, k ^ 1) for k in range(dp)]
    groups = [[2 * k + c for k in range(chips)] for c in range(2)]
    mr, nr = m // LANES, n // LANES
    sds = jax.ShapeDtypeStruct
    scores_t = sds((m, n), F32)
    row_t, col_t = sds((mr, LANES), F32), sds((nr, LANES), F32)
    row_parts_t, col_parts_t = sds((dp, mr, LANES), F32), sds((supp, nr, LANES), F32)
    wide_t = sds((chips, ROWS * (dim // LANES) + 8, LANES), F32)
    points_t = sds((chips, ROWS, dim), F32)
    row_s, col_s = pltpu.VMEM((m, LANES), F32), pltpu.VMEM((8, n), F32)

    def over_dp(parts):
        return lax.all_to_all(parts, "dp", 0, 0)

    def over_supp(parts):
        return lax.all_to_all(parts, "supp", 0, 0)

    weight = data_weight.reshape(nr, LANES)
    stack_t = sds((3 * n, dim), BF16)
    mass_s = pltpu.VMEM((8, LANES), F32)
    acc_s = pltpu.VMEM((m // 2, dim), F32)
    for update_step in range(OUTER):
        outs = (scores_t, scores_t, row_t, row_t, row_parts_t)
        scratch = [col_s, row_s, row_s]
        if update_step == 0:
            outs = outs + (sds((n, 3 * dim), BF16), col_t, col_t)
            scores, raw, row_norm, top, parts, wide_x, col_norm, shift = call(start_kernel, outs, scratch + [pltpu.VMEM((m, dim), F32), pltpu.VMEM((n, dim), F32), pltpu.SemaphoreType.DMA((5,))], "row0", inputs=pltpu.HBM, scale=scale)(*[pltpu.with_memory_space_constraint(v, pltpu.HBM) for v in (support_points, data_points)])
        else:
            scratch = scratch + [pltpu.VMEM((m, dim), F32)]
            scores, raw, row_norm, top, parts = call(next_row_kernel, outs, scratch, "row1", scale=scale)(own, other, wide_x, shift)
        parts = over_dp(parts)
        row_dual, parts = call(first_col_kernel, (row_t, col_parts_t), [row_s, pltpu.VMEM((mr, LANES), F32)], "col", log_support=-math.log2(total))(parts, row_norm, top, shift, scores, raw)
        parts = over_supp(parts)
        plan, col_dual, parts = call(next_row_sum_kernel, (scores_t, col_t, row_parts_t), [pltpu.VMEM((nr, LANES), F32), col_s, row_s, row_s], "plan")(parts, col_norm, weight, shift, scores, row_dual)
        parts = over_dp(parts)
        factor, parts = call(next_col_sum_kernel, (row_t, col_parts_t), [row_s], "colsum", share=1.0 / total)(parts, plan)
        parts = over_supp(parts)
        send, stack, ratio, shift = call(send_kernel, (wide_t, stack_t, col_t, col_t), [row_s, mass_s, acc_s], "send")(parts, weight, col_dual, col_norm, factor, plan, data_points)
        got = lax.ppermute(send, "dp", pairs)
        wide = call(keep_kernel, wide_t, [row_s, mass_s, acc_s], "keep")(ratio, factor, plan, stack)
        wide = call(add_kernel, wide_t, [], "add")(wide, got)
        wide = lax.all_to_all(wide, "dp", 0, 0, axis_index_groups=groups)
        own = call(divide_kernel, points_t, [pltpu.VMEM((LANES, LANES), F32)], "divide")(wide)
        own = lax.all_to_all(own, "dp", 0, 0, axis_index_groups=groups)
        other = lax.ppermute(own, "dp", pairs)
    halves = (own.reshape(m // 2, dim), other.reshape(m // 2, dim))
    return call(join_kernel, sds((m, dim), F32), [pltpu.SemaphoreType.DMA((2,))], "join", outputs=pltpu.HBM)(*halves)


def solution(mesh):
    return jax.shard_map(
        body,
        mesh=mesh,
        in_specs=(P("supp", None), P("dp", None), P("dp")),
        out_specs=P("supp", None),
        check_vma=False,
    )
```

```python
import math

import jax
import jax.numpy as jnp
from jax import lax
from jax.experimental import pallas as pl
from jax.experimental.pallas import tpu as pltpu
from jax.sharding import PartitionSpec as P

ITERS = 2
OUTER = 2
LANES = 128
ROWS = 64

F32 = jnp.float32
BF16 = jnp.bfloat16


def split(value):
    high = value.astype(BF16)
    low = (value - high.astype(F32)).astype(BF16)
    return high, low


def lane_row(block):
    return jnp.sum(block.T, axis=0, keepdims=True)


def spread_rows(vec_ref, out_ref):
    for a in range(vec_ref.shape[0]):
        block = jnp.broadcast_to(vec_ref[a : a + 1, :], (LANES, LANES))
        out_ref[a * LANES : (a + 1) * LANES, :] = block.T


def spread_cols(vec_ref, out_ref):
    for a in range(vec_ref.shape[0]):
        out_ref[:, a * LANES : (a + 1) * LANES] = jnp.broadcast_to(vec_ref[a : a + 1, :], (8, LANES))


def log_combine(parts):
    peak = jnp.max(parts, axis=0)
    return peak + jnp.log2(jnp.sum(jnp.exp2(parts - peak[None]), axis=0))


def tree(op, values):
    values = list(values)
    while len(values) > 1:
        values = [op(values[k], values[k + 1]) if k + 1 < len(values) else values[k] for k in range(0, len(values), 2)]
    return values[0]


def fold(block):
    return tree(jnp.add, [block[:, k : k + LANES] for k in range(0, block.shape[1], LANES)])


def prepare(x_ref, wide_ref, norm_ref, scale, start, count):
    dim = x_ref.shape[1]
    for a in range(start // LANES, (start + count) // LANES):
        rows = slice(a * LANES, (a + 1) * LANES)
        block = x_ref[rows, :]
        high, low = split(block)
        wide_ref[rows, :dim] = high
        wide_ref[rows, dim : 2 * dim] = high
        wide_ref[rows, 2 * dim :] = low
        norm_ref[a : a + 1, :] = lane_row(fold(block * block)) * scale


def score_half(points, wide_ref, cols_ref, put, peak_ref, scale, beside=None):
    high, low = split(points * (2.0 * scale))
    left = jnp.concatenate([high, low, high], axis=1)
    for k in range(0, wide_ref.shape[0], 512):
        acc = lax.dot_general(left, wide_ref[k : k + 512, :], (((1,), (1,)), ((), ())), preferred_element_type=F32)
        acc = acc + cols_ref[0:1, k : k + 512]
        put(k, acc)
        best = tree(jnp.maximum, [acc[:, q : q + LANES] for q in range(0, 512, LANES)])
        peak_ref[...] = best if k == 0 else jnp.maximum(peak_ref[...], best)
        if beside is not None:
            [beside(k // 256 + q) for q in range(2)]


def row_peaks(peak_ref, top_ref):
    for a in range(peak_ref.shape[0] // LANES):
        rows = slice(a * LANES, (a + 1) * LANES)
        top = jnp.max(peak_ref[rows, :].T, axis=0, keepdims=True)
        top_ref[a : a + 1, :] = top
        peak_ref[rows, :] = jnp.broadcast_to(top, (LANES, LANES)).T


def exp_rows(get, peak, plan_ref, rows, total_ref, total_rows):
    values = []
    for t in range(plan_ref.shape[1] // LANES):
        value = jnp.exp2(get(t) - peak)
        plan_ref[rows, t * LANES : (t + 1) * LANES] = value
        values.append(value)
    total_ref[total_rows, :] = tree(jnp.add, values)


def tile(t):
    return slice(t * LANES, (t + 1) * LANES)


def exp_loop(scores_ref, base, peak_ref, plan_ref, total_ref):
    def step(b, carry):
        for part in range(4):
            at = pl.ds(pl.multiple_of(b * 32 + part * 8, 8), 8)
            rows = pl.ds(pl.multiple_of(base + b * 32 + part * 8, 8), 8)
            exp_rows(lambda t: scores_ref[rows, tile(t)], peak_ref[at, :], plan_ref, rows, total_ref, at)
        return carry

    lax.fori_loop(0, peak_ref.shape[0] // 32, step, 0)


def finish_half(points, first, peak_top_ref, total_ref, norm_ref, top_ref, out_ref, scale):
    for a in range(total_ref.shape[0] // LANES):
        block = points(a)
        at = pl.ds(first + a, 1)
        top = peak_top_ref[a : a + 1, :]
        norm_ref[at, :] = lane_row(fold(block * block)) * scale
        top_ref[at, :] = top
        value = top + jnp.log2(lane_row(total_ref[tile(a), :]))
        for d in range(out_ref.shape[0]):
            out_ref[d, at, :] = value


def start_kernel(points_hbm, x_hbm, scores_ref, plan_ref, norm_ref, top_ref, out_ref, wide_ref, col_norm_ref, shift_ref, cols_ref, peak0_ref, peak1_ref, top0_ref, top1_ref, total0_ref, total1_ref, points_ref, x_ref, sems, *, scale):
    pieces = 4
    count = x_ref.shape[0] // pieces
    copies = [pltpu.make_async_copy(x_hbm.at[k * count : (k + 1) * count], x_ref.at[k * count : (k + 1) * count], sems.at[k]) for k in range(pieces)]
    copies.append(pltpu.make_async_copy(points_hbm, points_ref, sems.at[pieces]))
    for copy in copies:
        copy.start()
    for k in range(pieces):
        copies[k].wait()
        prepare(x_ref, wide_ref, col_norm_ref, scale, k * count, count)
    copies[pieces].wait()
    shift_ref[...] = -col_norm_ref[...]
    spread_cols(shift_ref, cols_ref)
    half = points_ref.shape[0] // 2
    groups = half // 8 // (wide_ref.shape[0] // 256)

    def put(start):
        def store(k, block):
            scores_ref[start : start + half, k : k + 512] = block

        return store

    def beside(k):
        for g in range(k * groups, (k + 1) * groups):
            rows = slice(g * 8, (g + 1) * 8)
            exp_rows(lambda t: scores_ref[rows, tile(t)], peak0_ref[rows, :], plan_ref, rows, total0_ref, rows)

    score_half(points_ref[:half, :], wide_ref, cols_ref, put(0), peak0_ref, scale)
    row_peaks(peak0_ref, top0_ref)
    score_half(points_ref[half:, :], wide_ref, cols_ref, put(half), peak1_ref, scale, beside)
    row_peaks(peak1_ref, top1_ref)
    exp_loop(scores_ref, half, peak1_ref, plan_ref, total1_ref)
    finish_half(lambda a: points_ref[tile(a), :], 0, top0_ref, total0_ref, norm_ref, top_ref, out_ref, scale)
    finish_half(lambda a: points_ref[half + a * LANES : half + (a + 1) * LANES, :], half // LANES, top1_ref, total1_ref, norm_ref, top_ref, out_ref, scale)


def own_row_kernel(own_ref, wide_ref, shift_ref, scores_ref, peak_ref, top_ref, cols_ref, *, scale):
    spread_cols(shift_ref, cols_ref)

    def put(k, block):
        scores_ref[:, k : k + 512] = block

    score_half(own_ref[...], wide_ref, cols_ref, put, peak_ref, scale)
    row_peaks(peak_ref, top_ref)


def other_row_kernel(own_ref, other_ref, wide_ref, shift_ref, own_scores_ref, peak0_ref, top0_ref, scores_ref, plan_ref, norm_ref, top_ref, out_ref, cols_ref, peak1_ref, top1_ref, total0_ref, total1_ref, *, scale):
    spread_cols(shift_ref, cols_ref)
    half = own_ref.shape[0]
    core = core_index()
    here = pl.multiple_of(core * half, half)
    there = pl.multiple_of((1 - core) * half, half)
    groups = half // 8 // (wide_ref.shape[0] // 256)

    def put(k, block):
        scores_ref[pl.ds(there, half), k : k + 512] = block

    def beside(k):
        for g in range(k * groups, (k + 1) * groups):
            rows = slice(g * 8, (g + 1) * 8)
            at = pl.ds(pl.multiple_of(here + g * 8, 8), 8)

            def get(t):
                value = own_scores_ref[rows, tile(t)]
                scores_ref[at, tile(t)] = value
                return value

            exp_rows(get, peak0_ref[rows, :], plan_ref, at, total0_ref, rows)

    score_half(other_ref[...], wide_ref, cols_ref, put, peak1_ref, scale, beside)
    row_peaks(peak1_ref, top1_ref)
    exp_loop(scores_ref, there, peak1_ref, plan_ref, total1_ref)
    blocks = half // LANES
    finish_half(lambda a: own_ref[tile(a), :], core * blocks, top0_ref, total0_ref, norm_ref, top_ref, out_ref, scale)
    finish_half(lambda a: other_ref[tile(a), :], (1 - core) * blocks, top1_ref, total1_ref, norm_ref, top_ref, out_ref, scale)


def core_index():
    return lax.axis_index("dp") % 2


def join_kernel(own_ref, other_ref, points_hbm, sems):
    half = own_ref.shape[0]
    core = core_index()
    first = pltpu.make_async_copy(own_ref, points_hbm.at[pl.ds(pl.multiple_of(core * half, half), half)], sems.at[0])
    second = pltpu.make_async_copy(other_ref, points_hbm.at[pl.ds(pl.multiple_of((1 - core) * half, half), half)], sems.at[1])
    first.start()
    second.start()
    first.wait()
    second.wait()


def column_sums(plan_ref, rows_ref):
    m, n = plan_ref.shape
    tiles = n // LANES

    def step(b, totals):
        totals = list(totals)
        for s in range(4):
            rows = pl.ds(pl.multiple_of(b * 32 + s * 8, 8), 8)
            u = rows_ref[rows, :]
            for t in range(tiles):
                totals[t] = totals[t] + plan_ref[rows, t * LANES : (t + 1) * LANES] * u
        return tuple(totals)

    totals = lax.fori_loop(0, m // 32, step, tuple(jnp.zeros((8, LANES), F32) for t in range(tiles)))
    return [jnp.sum(total, axis=0, keepdims=True) for total in totals]


def first_col_kernel(parts_ref, norm_ref, top_ref, shift_ref, scores_ref, plan_ref, dual_ref, out_ref, rows_ref, factor_ref, *, log_support):
    m, n = scores_ref.shape
    norm = norm_ref[...]
    log_total = log_combine(parts_ref[...]) - norm
    dual = (log_support - log_total) - norm
    dual_ref[...] = dual
    factor_ref[...] = jnp.exp2(dual + top_ref[...])
    spread_rows(factor_ref, rows_ref)
    sums = column_sums(plan_ref, rows_ref)
    for t, value in enumerate(sums):
        value = jnp.log2(value) - shift_ref[t : t + 1, :]
        for d in range(out_ref.shape[0]):
            out_ref[d, t : t + 1, :] = value

    @pl.when(jnp.min(tree(jnp.minimum, sums)) < 2.0**-80)
    def _():
        spread_rows(dual_ref, rows_ref)
        for t in range(n // LANES):
            cols = slice(t * LANES, (t + 1) * LANES)

            def top(b, peak):
                rows = pl.ds(pl.multiple_of(b * 8, 8), 8)
                return jnp.maximum(peak, scores_ref[rows, cols] + rows_ref[rows, :])

            peak = lax.fori_loop(0, m // 8, top, jnp.full((8, LANES), -jnp.inf, F32), unroll=8)
            best = jnp.max(peak, axis=0, keepdims=True)

            def add(b, total):
                rows = pl.ds(pl.multiple_of(b * 8, 8), 8)
                return total + jnp.exp2((scores_ref[rows, cols] + rows_ref[rows, :]) - best)

            total = lax.fori_loop(0, m // 8, add, jnp.zeros((8, LANES), F32), unroll=8)
            value = best + jnp.log2(jnp.sum(total, axis=0, keepdims=True)) - shift_ref[t : t + 1, :]
            for d in range(out_ref.shape[0]):
                out_ref[d, t : t + 1, :] = value


def next_row_sum_kernel(parts_ref, norm_ref, weight_ref, shift_ref, scores_ref, dual_ref, plan_ref, col_dual_ref, out_ref, delta_ref, cols_ref, rows_ref, total_ref):
    m, n = scores_ref.shape
    norm = norm_ref[...]
    col_dual = jnp.log2(weight_ref[...]) - (log_combine(parts_ref[...]) - norm)
    col_dual_ref[...] = col_dual
    delta_ref[...] = (col_dual - norm) - shift_ref[...]
    spread_cols(delta_ref, cols_ref)
    spread_rows(dual_ref, rows_ref)

    def step(b, carry):
        for half in range(4):
            rows = pl.ds(pl.multiple_of(b * 32 + half * 8, 8), 8)
            f = rows_ref[rows, :]
            plan = []
            for t in range(n // LANES):
                cols = slice(t * LANES, (t + 1) * LANES)
                value = jnp.exp2((scores_ref[rows, cols] + f) + cols_ref[:, cols])
                plan_ref[rows, cols] = value
                plan.append(value)
            total_ref[rows, :] = tree(jnp.add, plan)
        return carry

    lax.fori_loop(0, m // 32, step, 0)
    for a in range(m // LANES):
        value = lane_row(total_ref[a * LANES : (a + 1) * LANES, :])
        for d in range(out_ref.shape[0]):
            out_ref[d, a : a + 1, :] = value


def next_col_sum_kernel(parts_ref, plan_ref, factor_ref, out_ref, rows_ref, *, share):
    factor_ref[...] = share / jnp.sum(parts_ref[...], axis=0)
    spread_rows(factor_ref, rows_ref)
    for t, value in enumerate(column_sums(plan_ref, rows_ref)):
        for d in range(out_ref.shape[0]):
            out_ref[d, t : t + 1, :] = value


def move_half(half, plan_ref, factor_ref, ratio_ref, stack_ref, out_ref, rows_ref, mass_ref, acc_ref):
    n = plan_ref.shape[1]
    rows_here = plan_ref.shape[0] // 2
    spread_rows(factor_ref, rows_ref)
    stack = stack_ref[...]
    for b in range(rows_here // 256):
        at = pl.ds(pl.multiple_of(half * rows_here + b * 256, 256), 256)
        plan = plan_ref[at, :]
        left, rest = split(plan)
        acc = jnp.dot(jnp.concatenate([left, left, rest], axis=1), stack, preferred_element_type=F32)
        u = rows_ref[at, :]
        acc_ref[b * 256 : (b + 1) * 256, :] = acc * jnp.concatenate([u] * (acc.shape[1] // LANES), axis=1)
        mass = tree(jnp.add, [plan[:, t * LANES : (t + 1) * LANES] * ratio_ref[t : t + 1, :] for t in range(n // LANES)])
        mass = mass * u
        for a in range(2):
            mass_ref[2 * b + a : 2 * b + a + 1, :] = lane_row(mass[a * LANES : (a + 1) * LANES, :])
    tiles = acc_ref.shape[1] // LANES
    for d in range(out_ref.shape[0]):
        for t in range(tiles):
            out_ref[d, t * ROWS : (t + 1) * ROWS, :] = acc_ref[d * ROWS : (d + 1) * ROWS, t * LANES : (t + 1) * LANES]
        out_ref[d, tiles * ROWS :, :] = jnp.broadcast_to(mass_ref[d // 2 : d // 2 + 1, :], (8, LANES))


def send_kernel(parts_ref, weight_ref, col_dual_ref, norm_ref, factor_ref, plan_ref, x_ref, send_ref, stack_ref, ratio_ref, shift_ref, rows_ref, mass_ref, acc_ref):
    n = x_ref.shape[0]
    ratio_ref[...] = weight_ref[...] / jnp.sum(parts_ref[...], axis=0)
    shift_ref[...] = (col_dual_ref[...] + jnp.log2(ratio_ref[...])) - norm_ref[...]
    for a in range(0, n, LANES):
        v = jnp.broadcast_to(ratio_ref[a // LANES : a // LANES + 1, :], (LANES, LANES)).T
        high, low = split(x_ref[a : a + LANES, :] * jnp.concatenate([v] * (x_ref.shape[1] // LANES), axis=1))
        stack_ref[a : a + LANES, :] = high
        stack_ref[n + a : n + a + LANES, :] = low
        stack_ref[2 * n + a : 2 * n + a + LANES, :] = high
    move_half(1 - core_index(), plan_ref, factor_ref, ratio_ref, stack_ref, send_ref, rows_ref, mass_ref, acc_ref)


def keep_kernel(ratio_ref, factor_ref, plan_ref, stack_ref, out_ref, rows_ref, mass_ref, acc_ref):
    move_half(core_index(), plan_ref, factor_ref, ratio_ref, stack_ref, out_ref, rows_ref, mass_ref, acc_ref)


def add_kernel(a_ref, b_ref, out_ref):
    out_ref[...] = a_ref[...] + b_ref[...]


def divide_kernel(parts_ref, out_ref, mass_ref):
    parts = tree(jnp.add, [parts_ref[d] for d in range(parts_ref.shape[0])])
    tiles = out_ref.shape[2] // LANES
    mass_ref[...] = jnp.broadcast_to(parts[tiles * ROWS : tiles * ROWS + 1, :], (LANES, LANES)).T
    mass = mass_ref[pl.ds(pl.multiple_of((lax.axis_index("dp") // 2 % 2) * ROWS, ROWS), ROWS), :]
    points = jnp.concatenate([parts[t * ROWS : (t + 1) * ROWS, :] / mass for t in range(tiles)], axis=1)
    for d in range(out_ref.shape[0]):
        out_ref[d] = points


def call(kernel, outs, scratch, name, inputs=pltpu.VMEM, outputs=pltpu.VMEM, **params):
    def run(*args):
        return pl.pallas_call(
            (lambda *refs: kernel(*refs, **params)),
            out_shape=outs,
            in_specs=[pl.BlockSpec(memory_space=inputs)] * len(args),
            out_specs=jax.tree.map(lambda o: pl.BlockSpec(memory_space=outputs), outs),
            scratch_shapes=scratch,
            name=name,
            compiler_params=pltpu.CompilerParams(vmem_limit_bytes=20 * 1024 * 1024),
        )(*args)

    return run


def body(support_points, data_points, data_weight):
    m, dim = support_points.shape
    n = data_points.shape[0]
    dp = lax.axis_size("dp")
    supp = lax.axis_size("supp")
    epsilon = dim / 16.0
    scale = math.log2(math.e) / epsilon
    total = m * supp
    chips = dp // 2
    pairs = [(k, k ^ 1) for k in range(dp)]
    groups = [[2 * k + c for k in range(chips)] for c in range(2)]
    mr, nr = m // LANES, n // LANES
    sds = jax.ShapeDtypeStruct
    scores_t = sds((m, n), F32)
    row_t, col_t = sds((mr, LANES), F32), sds((nr, LANES), F32)
    row_parts_t, col_parts_t = sds((dp, mr, LANES), F32), sds((supp, nr, LANES), F32)
    wide_t = sds((chips, ROWS * (dim // LANES) + 8, LANES), F32)
    points_t = sds((chips, ROWS, dim), F32)
    row_s, col_s = pltpu.VMEM((m, LANES), F32), pltpu.VMEM((8, n), F32)

    def over_dp(parts):
        return lax.all_to_all(parts, "dp", 0, 0)

    def over_supp(parts):
        return lax.all_to_all(parts, "supp", 0, 0)

    weight = data_weight.reshape(nr, LANES)
    stack_t = sds((3 * n, dim), BF16)
    half_s, top_s = pltpu.VMEM((m // 2, LANES), F32), pltpu.VMEM((mr // 2, LANES), F32)
    mass_s = pltpu.VMEM((8, LANES), F32)
    acc_s = pltpu.VMEM((m // 2, dim), F32)
    for update_step in range(OUTER):
        outs = (scores_t, scores_t, row_t, row_t, row_parts_t)
        if update_step == 0:
            outs = outs + (sds((n, 3 * dim), BF16), col_t, col_t)
            scratch = [col_s, half_s, half_s, top_s, top_s, half_s, half_s, pltpu.VMEM((m, dim), F32), pltpu.VMEM((n, dim), F32), pltpu.SemaphoreType.DMA((5,))]
            held = [pltpu.with_memory_space_constraint(v, pltpu.HBM) for v in (support_points, data_points)]
            scores, raw, row_norm, top, parts, wide_x, col_norm, shift = call(start_kernel, outs, scratch, "row0", inputs=pltpu.HBM, scale=scale)(*held)
        else:
            own_outs = (sds((m // 2, n), F32), sds((m // 2, LANES), F32), sds((mr // 2, LANES), F32))
            early = call(own_row_kernel, own_outs, [col_s], "own", scale=scale)(own, wide_x, shift)
            scratch = [col_s, half_s, top_s, half_s, half_s]
            scores, raw, row_norm, top, parts = call(other_row_kernel, outs, scratch, "other", scale=scale)(own, other, wide_x, shift, *early)
        parts = over_dp(parts)
        row_dual, parts = call(first_col_kernel, (row_t, col_parts_t), [row_s, pltpu.VMEM((mr, LANES), F32)], "col", log_support=-math.log2(total))(parts, row_norm, top, shift, scores, raw)
        parts = over_supp(parts)
        plan, col_dual, parts = call(next_row_sum_kernel, (scores_t, col_t, row_parts_t), [pltpu.VMEM((nr, LANES), F32), col_s, row_s, row_s], "plan")(parts, col_norm, weight, shift, scores, row_dual)
        parts = over_dp(parts)
        factor, parts = call(next_col_sum_kernel, (row_t, col_parts_t), [row_s], "colsum", share=1.0 / total)(parts, plan)
        parts = over_supp(parts)
        send, stack, ratio, shift = call(send_kernel, (wide_t, stack_t, col_t, col_t), [row_s, mass_s, acc_s], "send")(parts, weight, col_dual, col_norm, factor, plan, data_points)
        got = lax.ppermute(send, "dp", pairs)
        wide = call(keep_kernel, wide_t, [row_s, mass_s, acc_s], "keep")(ratio, factor, plan, stack)
        wide = call(add_kernel, wide_t, [], "add")(wide, got)
        wide = lax.all_to_all(wide, "dp", 0, 0, axis_index_groups=groups)
        own = call(divide_kernel, points_t, [pltpu.VMEM((LANES, LANES), F32)], "divide")(wide)
        own = lax.all_to_all(own, "dp", 0, 0, axis_index_groups=groups)
        own = own.reshape(m // 2, dim)
        other = lax.ppermute(own, "dp", pairs)
    return call(join_kernel, sds((m, dim), F32), [pltpu.SemaphoreType.DMA((2,))], "join", outputs=pltpu.HBM)(own, other)


def solution(mesh):
    return jax.shard_map(
        body,
        mesh=mesh,
        in_specs=(P("supp", None), P("dp", None), P("dp")),
        out_specs=P("supp", None),
        check_vma=False,
    )
```

```python
import math

import jax
import jax.numpy as jnp
from jax import lax
from jax.experimental import pallas as pl
from jax.experimental.pallas import tpu as pltpu
from jax.sharding import PartitionSpec as P

ITERS = 2
OUTER = 2
LANES = 128
ROWS = 64

F32 = jnp.float32
BF16 = jnp.bfloat16


def split(value):
    high = value.astype(BF16)
    low = (value - high.astype(F32)).astype(BF16)
    return high, low


def lane_row(block):
    return jnp.sum(block.T, axis=0, keepdims=True)


def spread_rows(vec_ref, out_ref):
    for a in range(vec_ref.shape[0]):
        block = jnp.broadcast_to(vec_ref[a : a + 1, :], (LANES, LANES))
        out_ref[a * LANES : (a + 1) * LANES, :] = block.T


def spread_cols(vec_ref, out_ref):
    for a in range(vec_ref.shape[0]):
        out_ref[:, a * LANES : (a + 1) * LANES] = jnp.broadcast_to(vec_ref[a : a + 1, :], (8, LANES))


def log_combine(parts):
    peak = jnp.max(parts, axis=0)
    return peak + jnp.log2(jnp.sum(jnp.exp2(parts - peak[None]), axis=0))


def tree(op, values):
    values = list(values)
    while len(values) > 1:
        values = [op(values[k], values[k + 1]) if k + 1 < len(values) else values[k] for k in range(0, len(values), 2)]
    return values[0]


def fold(block):
    return tree(jnp.add, [block[:, k : k + LANES] for k in range(0, block.shape[1], LANES)])


def prepare(x_ref, wide_ref, norm_ref, scale, start, count):
    dim = x_ref.shape[1]
    for a in range(start // LANES, (start + count) // LANES):
        rows = slice(a * LANES, (a + 1) * LANES)
        block = x_ref[rows, :]
        high, low = split(block)
        wide_ref[rows, :dim] = high
        wide_ref[rows, dim : 2 * dim] = high
        wide_ref[rows, 2 * dim :] = low
        norm_ref[a : a + 1, :] = lane_row(fold(block * block)) * scale


def score_half(points, wide_ref, cols_ref, put, peak_ref, scale, beside=None):
    high, low = split(points * (2.0 * scale))
    left = jnp.concatenate([high, low, high], axis=1)
    for k in range(0, wide_ref.shape[0], 512):
        acc = lax.dot_general(left, wide_ref[k : k + 512, :], (((1,), (1,)), ((), ())), preferred_element_type=F32)
        acc = acc + cols_ref[0:1, k : k + 512]
        put(k, acc)
        best = tree(jnp.maximum, [acc[:, q : q + LANES] for q in range(0, 512, LANES)])
        peak_ref[...] = best if k == 0 else jnp.maximum(peak_ref[...], best)
        if beside is not None:
            [beside(k // 256 + q) for q in range(2)]


def row_peaks(peak_ref, top_ref):
    for a in range(peak_ref.shape[0] // LANES):
        rows = slice(a * LANES, (a + 1) * LANES)
        top = jnp.max(peak_ref[rows, :].T, axis=0, keepdims=True)
        top_ref[a : a + 1, :] = top
        peak_ref[rows, :] = jnp.broadcast_to(top, (LANES, LANES)).T


def exp_rows(get, peak, plan_ref, rows, total_ref, total_rows):
    values = []
    for t in range(plan_ref.shape[1] // LANES):
        value = jnp.exp2(get(t) - peak)
        plan_ref[rows, t * LANES : (t + 1) * LANES] = value
        values.append(value)
    total_ref[total_rows, :] = tree(jnp.add, values)


def tile(t):
    return slice(t * LANES, (t + 1) * LANES)


def exp_loop(scores_ref, base, peak_ref, plan_ref, total_ref):
    def step(b, carry):
        for part in range(4):
            at = pl.ds(pl.multiple_of(b * 32 + part * 8, 8), 8)
            rows = pl.ds(pl.multiple_of(base + b * 32 + part * 8, 8), 8)
            exp_rows(lambda t: scores_ref[rows, tile(t)], peak_ref[at, :], plan_ref, rows, total_ref, at)
        return carry

    lax.fori_loop(0, peak_ref.shape[0] // 32, step, 0)


def finish_half(points, first, peak_top_ref, total_ref, norm_ref, top_ref, out_ref, scale):
    for a in range(total_ref.shape[0] // LANES):
        block = points(a)
        at = pl.ds(first + a, 1)
        top = peak_top_ref[a : a + 1, :]
        norm_ref[at, :] = lane_row(fold(block * block)) * scale
        top_ref[at, :] = top
        value = top + jnp.log2(lane_row(total_ref[tile(a), :]))
        for d in range(out_ref.shape[0]):
            out_ref[d, at, :] = value


def start_kernel(points_hbm, x_hbm, scores_ref, plan_ref, norm_ref, top_ref, out_ref, wide_ref, col_norm_ref, shift_ref, x_ref, cols_ref, peak0_ref, peak1_ref, top0_ref, top1_ref, total0_ref, total1_ref, points_ref, sems, *, scale):
    pieces = 4
    count = x_ref.shape[0] // pieces
    copies = [pltpu.make_async_copy(x_hbm.at[k * count : (k + 1) * count], x_ref.at[k * count : (k + 1) * count], sems.at[k]) for k in range(pieces)]
    copies.append(pltpu.make_async_copy(points_hbm, points_ref, sems.at[pieces]))
    for copy in copies:
        copy.start()
    for k in range(pieces):
        copies[k].wait()
        prepare(x_ref, wide_ref, col_norm_ref, scale, k * count, count)
    copies[pieces].wait()
    shift_ref[...] = -col_norm_ref[...]
    spread_cols(shift_ref, cols_ref)
    half = points_ref.shape[0] // 2
    groups = half // 8 // (wide_ref.shape[0] // 256)

    def put(start):
        def store(k, block):
            scores_ref[start : start + half, k : k + 512] = block

        return store

    def beside(k):
        for g in range(k * groups, (k + 1) * groups):
            rows = slice(g * 8, (g + 1) * 8)
            exp_rows(lambda t: scores_ref[rows, tile(t)], peak0_ref[rows, :], plan_ref, rows, total0_ref, rows)

    score_half(points_ref[:half, :], wide_ref, cols_ref, put(0), peak0_ref, scale)
    row_peaks(peak0_ref, top0_ref)
    score_half(points_ref[half:, :], wide_ref, cols_ref, put(half), peak1_ref, scale, beside)
    row_peaks(peak1_ref, top1_ref)
    exp_loop(scores_ref, half, peak1_ref, plan_ref, total1_ref)
    finish_half(lambda a: points_ref[tile(a), :], 0, top0_ref, total0_ref, norm_ref, top_ref, out_ref, scale)
    finish_half(lambda a: points_ref[half + a * LANES : half + (a + 1) * LANES, :], half // LANES, top1_ref, total1_ref, norm_ref, top_ref, out_ref, scale)


def own_row_kernel(own_ref, wide_ref, shift_ref, scores_ref, peak_ref, top_ref, cols_ref, *, scale):
    spread_cols(shift_ref, cols_ref)

    def put(k, block):
        scores_ref[:, k : k + 512] = block

    score_half(own_ref[...], wide_ref, cols_ref, put, peak_ref, scale)
    row_peaks(peak_ref, top_ref)


def other_row_kernel(own_ref, other_ref, wide_ref, shift_ref, own_scores_ref, peak0_ref, top0_ref, scores_ref, plan_ref, norm_ref, top_ref, out_ref, cols_ref, peak1_ref, top1_ref, total0_ref, total1_ref, *, scale):
    spread_cols(shift_ref, cols_ref)
    half = own_ref.shape[0]
    core = core_index()
    here = pl.multiple_of(core * half, half)
    there = pl.multiple_of((1 - core) * half, half)
    groups = half // 8 // (wide_ref.shape[0] // 256)

    def put(k, block):
        scores_ref[pl.ds(there, half), k : k + 512] = block

    def beside(k):
        for g in range(k * groups, (k + 1) * groups):
            rows = slice(g * 8, (g + 1) * 8)
            at = pl.ds(pl.multiple_of(here + g * 8, 8), 8)

            def get(t):
                value = own_scores_ref[rows, tile(t)]
                scores_ref[at, tile(t)] = value
                return value

            exp_rows(get, peak0_ref[rows, :], plan_ref, at, total0_ref, rows)

    score_half(other_ref[...], wide_ref, cols_ref, put, peak1_ref, scale, beside)
    row_peaks(peak1_ref, top1_ref)
    exp_loop(scores_ref, there, peak1_ref, plan_ref, total1_ref)
    blocks = half // LANES
    finish_half(lambda a: own_ref[tile(a), :], core * blocks, top0_ref, total0_ref, norm_ref, top_ref, out_ref, scale)
    finish_half(lambda a: other_ref[tile(a), :], (1 - core) * blocks, top1_ref, total1_ref, norm_ref, top_ref, out_ref, scale)


def core_index():
    return lax.axis_index("dp") % 2


def join_kernel(own_ref, other_ref, points_hbm, sems):
    half = own_ref.shape[0]
    core = core_index()
    first = pltpu.make_async_copy(own_ref, points_hbm.at[pl.ds(pl.multiple_of(core * half, half), half)], sems.at[0])
    second = pltpu.make_async_copy(other_ref, points_hbm.at[pl.ds(pl.multiple_of((1 - core) * half, half), half)], sems.at[1])
    first.start()
    second.start()
    first.wait()
    second.wait()


def column_sums(plan_ref, rows_ref):
    m, n = plan_ref.shape
    tiles = n // LANES

    def step(b, totals):
        totals = list(totals)
        for s in range(4):
            rows = pl.ds(pl.multiple_of(b * 32 + s * 8, 8), 8)
            u = rows_ref[rows, :]
            for t in range(tiles):
                totals[t] = totals[t] + plan_ref[rows, t * LANES : (t + 1) * LANES] * u
        return tuple(totals)

    totals = lax.fori_loop(0, m // 32, step, tuple(jnp.zeros((8, LANES), F32) for t in range(tiles)))
    return [jnp.sum(total, axis=0, keepdims=True) for total in totals]


def first_col_kernel(parts_ref, norm_ref, top_ref, shift_ref, scores_ref, plan_ref, dual_ref, out_ref, rows_ref, factor_ref, *, log_support):
    m, n = scores_ref.shape
    norm = norm_ref[...]
    log_total = log_combine(parts_ref[...]) - norm
    dual = (log_support - log_total) - norm
    dual_ref[...] = dual
    factor_ref[...] = jnp.exp2(dual + top_ref[...])
    spread_rows(factor_ref, rows_ref)
    sums = column_sums(plan_ref, rows_ref)
    for t, value in enumerate(sums):
        value = jnp.log2(value) - shift_ref[t : t + 1, :]
        for d in range(out_ref.shape[0]):
            out_ref[d, t : t + 1, :] = value

    @pl.when(jnp.min(tree(jnp.minimum, sums)) < 2.0**-80)
    def _():
        spread_rows(dual_ref, rows_ref)
        for t in range(n // LANES):
            cols = slice(t * LANES, (t + 1) * LANES)

            def top(b, peak):
                rows = pl.ds(pl.multiple_of(b * 8, 8), 8)
                return jnp.maximum(peak, scores_ref[rows, cols] + rows_ref[rows, :])

            peak = lax.fori_loop(0, m // 8, top, jnp.full((8, LANES), -jnp.inf, F32), unroll=8)
            best = jnp.max(peak, axis=0, keepdims=True)

            def add(b, total):
                rows = pl.ds(pl.multiple_of(b * 8, 8), 8)
                return total + jnp.exp2((scores_ref[rows, cols] + rows_ref[rows, :]) - best)

            total = lax.fori_loop(0, m // 8, add, jnp.zeros((8, LANES), F32), unroll=8)
            value = best + jnp.log2(jnp.sum(total, axis=0, keepdims=True)) - shift_ref[t : t + 1, :]
            for d in range(out_ref.shape[0]):
                out_ref[d, t : t + 1, :] = value


def next_row_sum_kernel(parts_ref, norm_ref, weight_ref, shift_ref, scores_ref, dual_ref, plan_ref, col_dual_ref, out_ref, delta_ref, cols_ref, rows_ref, total_ref):
    m, n = scores_ref.shape
    norm = norm_ref[...]
    col_dual = jnp.log2(weight_ref[...]) - (log_combine(parts_ref[...]) - norm)
    col_dual_ref[...] = col_dual
    delta_ref[...] = (col_dual - norm) - shift_ref[...]
    spread_cols(delta_ref, cols_ref)
    spread_rows(dual_ref, rows_ref)

    def step(b, carry):
        for half in range(4):
            rows = pl.ds(pl.multiple_of(b * 32 + half * 8, 8), 8)
            f = rows_ref[rows, :]
            plan = []
            for t in range(n // LANES):
                cols = slice(t * LANES, (t + 1) * LANES)
                value = jnp.exp2((scores_ref[rows, cols] + f) + cols_ref[:, cols])
                plan_ref[rows, cols] = value
                plan.append(value)
            total_ref[rows, :] = tree(jnp.add, plan)
        return carry

    lax.fori_loop(0, m // 32, step, 0)
    for a in range(m // LANES):
        value = lane_row(total_ref[a * LANES : (a + 1) * LANES, :])
        for d in range(out_ref.shape[0]):
            out_ref[d, a : a + 1, :] = value


def next_col_sum_kernel(parts_ref, plan_ref, factor_ref, out_ref, rows_ref, *, share):
    factor_ref[...] = share / jnp.sum(parts_ref[...], axis=0)
    spread_rows(factor_ref, rows_ref)
    for t, value in enumerate(column_sums(plan_ref, rows_ref)):
        for d in range(out_ref.shape[0]):
            out_ref[d, t : t + 1, :] = value


def move_half(half, plan_ref, factor_ref, ratio_ref, stack_ref, out_ref, rows_ref, mass_ref, acc_ref):
    n = plan_ref.shape[1]
    rows_here = plan_ref.shape[0] // 2
    spread_rows(factor_ref, rows_ref)
    stack = stack_ref[...]
    for b in range(rows_here // 256):
        at = pl.ds(pl.multiple_of(half * rows_here + b * 256, 256), 256)
        plan = plan_ref[at, :]
        left, rest = split(plan)
        acc = jnp.dot(jnp.concatenate([left, left, rest], axis=1), stack, preferred_element_type=F32)
        u = rows_ref[at, :]
        acc_ref[b * 256 : (b + 1) * 256, :] = acc * jnp.concatenate([u] * (acc.shape[1] // LANES), axis=1)
        mass = tree(jnp.add, [plan[:, t * LANES : (t + 1) * LANES] * ratio_ref[t : t + 1, :] for t in range(n // LANES)])
        mass = mass * u
        for a in range(2):
            mass_ref[2 * b + a : 2 * b + a + 1, :] = lane_row(mass[a * LANES : (a + 1) * LANES, :])
    tiles = acc_ref.shape[1] // LANES
    for d in range(out_ref.shape[0]):
        for t in range(tiles):
            out_ref[d, t * ROWS : (t + 1) * ROWS, :] = acc_ref[d * ROWS : (d + 1) * ROWS, t * LANES : (t + 1) * LANES]
        out_ref[d, tiles * ROWS :, :] = jnp.broadcast_to(mass_ref[d // 2 : d // 2 + 1, :], (8, LANES))


def send_kernel(parts_ref, weight_ref, col_dual_ref, norm_ref, factor_ref, plan_ref, x_ref, send_ref, stack_ref, ratio_ref, shift_ref, rows_ref, mass_ref, acc_ref):
    n = x_ref.shape[0]
    ratio_ref[...] = weight_ref[...] / jnp.sum(parts_ref[...], axis=0)
    shift_ref[...] = (col_dual_ref[...] + jnp.log2(ratio_ref[...])) - norm_ref[...]
    for a in range(0, n, LANES):
        v = jnp.broadcast_to(ratio_ref[a // LANES : a // LANES + 1, :], (LANES, LANES)).T
        high, low = split(x_ref[a : a + LANES, :] * jnp.concatenate([v] * (x_ref.shape[1] // LANES), axis=1))
        stack_ref[a : a + LANES, :] = high
        stack_ref[n + a : n + a + LANES, :] = low
        stack_ref[2 * n + a : 2 * n + a + LANES, :] = high
    move_half(1 - core_index(), plan_ref, factor_ref, ratio_ref, stack_ref, send_ref, rows_ref, mass_ref, acc_ref)


def keep_kernel(ratio_ref, factor_ref, plan_ref, stack_ref, out_ref, rows_ref, mass_ref, acc_ref):
    move_half(core_index(), plan_ref, factor_ref, ratio_ref, stack_ref, out_ref, rows_ref, mass_ref, acc_ref)


def add_kernel(a_ref, b_ref, out_ref):
    out_ref[...] = a_ref[...] + b_ref[...]


def divide_kernel(parts_ref, out_ref, mass_ref):
    parts = tree(jnp.add, [parts_ref[d] for d in range(parts_ref.shape[0])])
    tiles = out_ref.shape[2] // LANES
    mass_ref[...] = jnp.broadcast_to(parts[tiles * ROWS : tiles * ROWS + 1, :], (LANES, LANES)).T
    mass = mass_ref[pl.ds(pl.multiple_of((lax.axis_index("dp") // 2 % 2) * ROWS, ROWS), ROWS), :]
    points = jnp.concatenate([parts[t * ROWS : (t + 1) * ROWS, :] / mass for t in range(tiles)], axis=1)
    for d in range(out_ref.shape[0]):
        out_ref[d] = points


def call(kernel, outs, scratch, name, inputs=pltpu.VMEM, outputs=pltpu.VMEM, **params):
    def run(*args):
        return pl.pallas_call(
            (lambda *refs: kernel(*refs, **params)),
            out_shape=outs,
            in_specs=[pl.BlockSpec(memory_space=inputs)] * len(args),
            out_specs=jax.tree.map(lambda o: pl.BlockSpec(memory_space=outputs), outs),
            scratch_shapes=scratch,
            name=name,
            compiler_params=pltpu.CompilerParams(vmem_limit_bytes=20 * 1024 * 1024),
        )(*args)

    return run


def body(support_points, data_points, data_weight):
    m, dim = support_points.shape
    n = data_points.shape[0]
    dp = lax.axis_size("dp")
    supp = lax.axis_size("supp")
    epsilon = dim / 16.0
    scale = math.log2(math.e) / epsilon
    total = m * supp
    chips = dp // 2
    pairs = [(k, k ^ 1) for k in range(dp)]
    groups = [[2 * k + c for k in range(chips)] for c in range(2)]
    mr, nr = m // LANES, n // LANES
    sds = jax.ShapeDtypeStruct
    scores_t = sds((m, n), F32)
    row_t, col_t = sds((mr, LANES), F32), sds((nr, LANES), F32)
    row_parts_t, col_parts_t = sds((dp, mr, LANES), F32), sds((supp, nr, LANES), F32)
    wide_t = sds((chips, ROWS * (dim // LANES) + 8, LANES), F32)
    points_t = sds((chips, ROWS, dim), F32)
    row_s, col_s = pltpu.VMEM((m, LANES), F32), pltpu.VMEM((8, n), F32)

    def over_dp(parts):
        return lax.all_to_all(parts, "dp", 0, 0)

    def over_supp(parts):
        return lax.all_to_all(parts, "supp", 0, 0)

    weight = data_weight.reshape(nr, LANES)
    stack_t = sds((3 * n, dim), BF16)
    half_s, top_s = pltpu.VMEM((m // 2, LANES), F32), pltpu.VMEM((mr // 2, LANES), F32)
    mass_s = pltpu.VMEM((8, LANES), F32)
    acc_s = pltpu.VMEM((m // 2, dim), F32)
    for update_step in range(OUTER):
        outs = (scores_t, scores_t, row_t, row_t, row_parts_t)
        if update_step == 0:
            outs = outs + (sds((n, 3 * dim), BF16), col_t, col_t, sds((n, dim), F32))
            scratch = [col_s, half_s, half_s, top_s, top_s, half_s, half_s, pltpu.VMEM((m, dim), F32), pltpu.SemaphoreType.DMA((5,))]
            held = [pltpu.with_memory_space_constraint(v, pltpu.HBM) for v in (support_points, data_points)]
            scores, raw, row_norm, top, parts, wide_x, col_norm, shift, data = call(start_kernel, outs, scratch, "row0", inputs=pltpu.HBM, scale=scale)(*held)
        else:
            own_outs = (sds((m // 2, n), F32), sds((m // 2, LANES), F32), sds((mr // 2, LANES), F32))
            early = call(own_row_kernel, own_outs, [col_s], "own", scale=scale)(own, wide_x, shift)
            scratch = [col_s, half_s, top_s, half_s, half_s]
            scores, raw, row_norm, top, parts = call(other_row_kernel, outs, scratch, "other", scale=scale)(own, other, wide_x, shift, *early)
        parts = over_dp(parts)
        row_dual, parts = call(first_col_kernel, (row_t, col_parts_t), [row_s, pltpu.VMEM((mr, LANES), F32)], "col", log_support=-math.log2(total))(parts, row_norm, top, shift, scores, raw)
        parts = over_supp(parts)
        plan, col_dual, parts = call(next_row_sum_kernel, (scores_t, col_t, row_parts_t), [pltpu.VMEM((nr, LANES), F32), col_s, row_s, row_s], "plan")(parts, col_norm, weight, shift, scores, row_dual)
        parts = over_dp(parts)
        factor, parts = call(next_col_sum_kernel, (row_t, col_parts_t), [row_s], "colsum", share=1.0 / total)(parts, plan)
        parts = over_supp(parts)
        send, stack, ratio, shift = call(send_kernel, (wide_t, stack_t, col_t, col_t), [row_s, mass_s, acc_s], "send")(parts, weight, col_dual, col_norm, factor, plan, data)
        got = lax.ppermute(send, "dp", pairs)
        wide = call(keep_kernel, wide_t, [row_s, mass_s, acc_s], "keep")(ratio, factor, plan, stack)
        wide = call(add_kernel, wide_t, [], "add")(wide, got)
        wide = lax.all_to_all(wide, "dp", 0, 0, axis_index_groups=groups)
        own = call(divide_kernel, points_t, [pltpu.VMEM((LANES, LANES), F32)], "divide")(wide)
        own = lax.all_to_all(own, "dp", 0, 0, axis_index_groups=groups)
        own = own.reshape(m // 2, dim)
        other = lax.ppermute(own, "dp", pairs)
    return call(join_kernel, sds((m, dim), F32), [pltpu.SemaphoreType.DMA((2,))], "join", outputs=pltpu.HBM)(own, other)


def solution(mesh):
    return jax.shard_map(
        body,
        mesh=mesh,
        in_specs=(P("supp", None), P("dp", None), P("dp")),
        out_specs=P("supp", None),
        check_vma=False,
    )
```
